256 devices in a mesh: dom: 16 (over y, x), sub: 16 (over z, core).
Axes of the slice: x: 4, y: 4, z: 8, core: 2. Of those that a mesh axis runs over, the one named last changes fastest.
Arguments:
- coords: float32 [3, 65536], P(None, ('dom', 'sub')), may hold values from -6 to 6
- direction: float32 [3, 65536], P(None, ('dom', 'sub')), may hold values from -6 to 6
- connect: int32 [4, 262144], P(None, ('dom', 'sub')), may hold values from 0 to 383
- shape_inv: float32 [9, 262144], P(None, ('dom', 'sub')), may hold values from -3.5 to 3.5
- weight: float32 [262144], P(('dom', 'sub')), may hold values from 0.3 to 9
- send_node: int32 [256, 128], P(('dom', 'sub')), may hold values from 0 to 255
- recv_slot: int32 [256, 128], P(('dom', 'sub')), may hold values from 0 to 127, each once within a row
Outputs:
- gradient: float32 [4, 3, 65536], P(None, None, ('dom', 'sub'))
- energy: float32 [4], replicated
- min_det: float32 [4], replicated
The draws below stay inside these ranges and needn't reach their ends.
Inputs may be any that keep to these rules, and one draw needn't show every extreme that they name: `connect`: each tetrahedron's corners are local node numbers: owned nodes below 256, ghost slots above. `send_node`: owned node numbers; a node may be listed several times. `recv_slot`: each row is a permutation of the ghost slots.
All inputs are finite; a program needn't handle non-finite values.
Results may differ from the reference program's by a relative error of at most 0.0001.
Values sent between devices are 32-bit elements; how exact they have to be, the bound alone decides.
A program may use at most 64 MiB of HBM per device.

```python
import math
import jax
import jax.numpy as jnp
from jax import lax

NODE_DEV = 256
TRIALS = 4
ELEM_DEV = 1024
SHARE = 32
GHOST_DEV = 128
NODES = 65536
ELEMS = 262144
N_DOM = 16
N_SUB = 16


def draw_weight(key, part):
    total_elems = ELEM_DEV * N_DOM * N_SUB
    device = (jnp.arange(total_elems) // ELEM_DEV).astype(jnp.float32)
    rising = 1.0 + 2.0 * device / max(N_DOM * N_SUB - 1, 1)
    base_value = jnp.exp(jax.random.uniform(key, (total_elems,), jnp.float32, math.log(0.5), math.log(2.0)))
    return base_value * rising


def with_ends(entries, rng, least, high):
    longest = entries.shape.index(max(entries.shape))
    spots = []
    for shift in (0, 1):
        where = [jax.random.randint(jax.random.fold_in(rng, axis), (), 0, length) for axis, length in enumerate(entries.shape)]
        where[longest] = (where[longest] + shift) % entries.shape[longest]
        spots.append(tuple(where))
    return entries.at[spots[0]].set(least).at[spots[1]].set(high)


def level_of(stream_key, shape, split, least, high):
    def one(position, shards_of):
        steps = jax.random.uniform(jax.random.fold_in(jax.random.fold_in(stream_key, 6), position), (shards_of,), jnp.float32, least / len(split), high / len(split))
        return jnp.repeat(jnp.exp(steps), shape[position] // shards_of).reshape((-1,) + (1,) * (len(shape) - position - 1))

    level = one(*split[0])
    for cut in split[1:]:
        level = level * one(*cut)
    return level


def noise(rng, dims, scale, bound, shards=(), held_as=jnp.bfloat16):
    drawn = scale * jax.random.normal(rng, dims, jnp.float32)
    if shards:
        drawn = drawn * level_of(rng, dims, shards, -0.22, 0.18)
    return jnp.clip(drawn, -bound, bound).astype(held_as)


def setup_inputs(seed: int = 0) -> dict:
    keys = jax.random.split(jax.random.key(seed), 8)
    return {
        "coords": noise(keys[0], (3, NODES), 1.0, 6.0, ((1, 256),), jnp.float32),
        "direction": noise(keys[1], (3, NODES), 0.5, 6.0, ((1, 256),), jnp.float32),
        "connect": with_ends(jax.random.randint(keys[2], (4, ELEMS), 0, NODE_DEV + GHOST_DEV), jax.random.fold_in(keys[2], 1), 0, (NODE_DEV + GHOST_DEV) - 1).astype(jnp.int32),
        "shape_inv": noise(keys[3], (9, ELEMS), 3 ** -0.5, 3.5, ((1, 256),), jnp.float32),
        "weight": draw_weight(jax.random.fold_in(keys[7], 71), 0),
        "send_node": with_ends(jax.random.randint(keys[5], (N_DOM * N_SUB, GHOST_DEV), 0, NODE_DEV), jax.random.fold_in(keys[5], 1), 0, NODE_DEV - 1).astype(jnp.int32),
        "recv_slot": jax.vmap(lambda own: jax.random.permutation(own, GHOST_DEV))(jax.random.split(keys[6], (N_DOM * N_SUB))).reshape((N_DOM * N_SUB, GHOST_DEV)).astype(jnp.int32),
    }


step_scales = (1.0, 0.5, 0.25, 0.125)

def jacobian(places, connect, shape_inv):
    elem_count = connect.shape[1]
    corners_all = jnp.take(places, connect.reshape(-1), axis=1).reshape(3, 4, elem_count)
    differ = corners_all[:, 1:] - corners_all[:, :1]
    return [[differ[row_index, 0] * shape_inv[col_index] + differ[row_index, 1] * shape_inv[3 + col_index] + differ[row_index, 2] * shape_inv[6 + col_index] for col_index in range(3)] for row_index in range(3)]

def cofactor(matrix):
    return [[matrix[1][1] * matrix[2][2] - matrix[1][2] * matrix[2][1], matrix[1][2] * matrix[2][0] - matrix[1][0] * matrix[2][2], matrix[1][0] * matrix[2][1] - matrix[1][1] * matrix[2][0]], [matrix[0][2] * matrix[2][1] - matrix[0][1] * matrix[2][2], matrix[0][0] * matrix[2][2] - matrix[0][2] * matrix[2][0], matrix[0][1] * matrix[2][0] - matrix[0][0] * matrix[2][1]], [matrix[0][1] * matrix[1][2] - matrix[0][2] * matrix[1][1], matrix[0][2] * matrix[1][0] - matrix[0][0] * matrix[1][2], matrix[0][0] * matrix[1][1] - matrix[0][1] * matrix[1][0]]]

def element_dets(places, connect, shape_inv):
    matrix = jacobian(places, connect, shape_inv)
    cofac = cofactor(matrix)
    return matrix[0][0] * cofac[0][0] + matrix[0][1] * cofac[0][1] + matrix[0][2] * cofac[0][2]

def barrier_shift(lowest):
    return lowest - 1.0 - jnp.abs(lowest)

def element_grad(places, connect, shape_inv, weight, shift, node_count):
    matrix = jacobian(places, connect, shape_inv)
    cofac = cofactor(matrix)
    determ = matrix[0][0] * cofac[0][0] + matrix[0][1] * cofac[0][1] + matrix[0][2] * cofac[0][2]
    lifted = determ - shift
    squares = matrix[0][0] * matrix[0][0]
    for row_index in range(3):
        for col_index in range(3):
            if row_index + col_index > 0:
                squares = squares + matrix[row_index][col_index] * matrix[row_index][col_index]
    power = lifted ** (-2.0 / 3.0)
    energy_part = jnp.sum(weight * squares * power) / 3.0
    scale_jac = weight * power * (2.0 / 3.0)
    scale_cof = weight * squares * power / lifted * (2.0 / 9.0)
    djac = [[scale_jac * matrix[row_index][col_index] - scale_cof * cofac[row_index][col_index] for col_index in range(3)] for row_index in range(3)]
    flat_index = connect.reshape(-1)
    rows_out = []
    for row_index in range(3):
        dedge = [djac[row_index][0] * shape_inv[3 * edge_index] + djac[row_index][1] * shape_inv[3 * edge_index + 1] + djac[row_index][2] * shape_inv[3 * edge_index + 2] for edge_index in range(3)]
        rows_out.append(jnp.concatenate([-(dedge[0] + dedge[1] + dedge[2]), dedge[0], dedge[1], dedge[2]]))
    combined = jnp.stack(rows_out)
    targets = flat_index[None, :] + node_count * jnp.arange(3, dtype=jnp.int32)[:, None]
    summed = jax.ops.segment_sum(combined.reshape(-1), targets.reshape(-1), num_segments=3 * node_count)
    return (energy_part, summed.reshape(3, node_count))

def reference(coords, direction, connect, shape_inv, weight, send_node, recv_slot):
    devices_all = N_DOM * N_SUB
    local_count = NODE_DEV + GHOST_DEV
    both = jnp.concatenate([coords, direction], axis=0).reshape(6, devices_all, NODE_DEV).transpose(1, 0, 2)
    outgoing = jax.vmap(lambda rows, picks: jnp.take(rows, picks, axis=1))(both, send_node)
    outgoing = outgoing.reshape(N_DOM, N_SUB, 6, 4, SHARE)
    arrived = jnp.stack([jnp.roll(outgoing[:, :, :, 0], 1, axis=0), jnp.roll(outgoing[:, :, :, 1], -1, axis=0), jnp.roll(outgoing[:, :, :, 2], 1, axis=1), jnp.roll(outgoing[:, :, :, 3], -1, axis=1)], axis=3)
    arrived = arrived.reshape(devices_all, 6, GHOST_DEV)
    ghosts = jax.vmap(lambda rows, slots: jnp.zeros_like(rows).at[:, slots].set(rows))(arrived, recv_slot)
    local = jnp.concatenate([both, ghosts], axis=2)

    def device_lows(device):
        local_rows = local[device]
        connect_dev = lax.dynamic_slice_in_dim(connect, device * ELEM_DEV, ELEM_DEV, 1)
        inverse_dev = lax.dynamic_slice_in_dim(shape_inv, device * ELEM_DEV, ELEM_DEV, 1)
        lows = [jnp.min(element_dets(local_rows[:3] + step_scales[trial_index] * local_rows[3:], connect_dev, inverse_dev)) for trial_index in range(TRIALS)]
        return jnp.stack(lows)
    lows = lax.map(device_lows, jnp.arange(devices_all, dtype=jnp.int32))
    lowest = lax.optimization_barrier(jnp.min(lows, axis=0))
    shifts = barrier_shift(lowest)

    def device_terms(device):
        local_rows = local[device]
        connect_dev = lax.dynamic_slice_in_dim(connect, device * ELEM_DEV, ELEM_DEV, 1)
        inverse_dev = lax.dynamic_slice_in_dim(shape_inv, device * ELEM_DEV, ELEM_DEV, 1)
        weight_dev = lax.dynamic_slice_in_dim(weight, device * ELEM_DEV, ELEM_DEV, 0)
        parts = []
        grads = []
        for trial_index in range(TRIALS):
            places = local_rows[:3] + step_scales[trial_index] * local_rows[3:]
            energy_part, grad_rows = element_grad(places, connect_dev, inverse_dev, weight_dev, shifts[trial_index], local_count)
            parts.append(energy_part)
            grads.append(grad_rows)
        return (jnp.stack(parts), jnp.stack(grads))
    parts, grads = lax.map(device_terms, jnp.arange(devices_all, dtype=jnp.int32))
    energy = lax.optimization_barrier(jnp.sum(parts, axis=0)) / (ELEM_DEV * devices_all)
    owned = grads[..., :NODE_DEV]
    ghost_grads = grads[..., NODE_DEV:]
    returned = jax.vmap(lambda rows, slots: rows[..., slots])(ghost_grads, recv_slot).reshape(N_DOM, N_SUB, TRIALS, 3, 4, SHARE)
    back_rows = jnp.stack([jnp.roll(returned[:, :, :, :, 0], -1, axis=0), jnp.roll(returned[:, :, :, :, 1], 1, axis=0), jnp.roll(returned[:, :, :, :, 2], -1, axis=1), jnp.roll(returned[:, :, :, :, 3], 1, axis=1)], axis=4)
    back_rows = back_rows.reshape(devices_all, TRIALS, 3, GHOST_DEV)
    owned = jax.vmap(lambda rows, picks, extra: rows.at[..., picks].add(extra))(owned, send_node, back_rows)
    gradient = owned.transpose(1, 2, 0, 3).reshape(TRIALS, 3, NODE_DEV * devices_all)
    return (gradient, energy, lowest)
```

```python
import functools

import jax
import jax.numpy as jnp
from jax import lax
from jax.experimental import pallas as pl
from jax.experimental.pallas import tpu as pltpu
from jax.sharding import PartitionSpec as P

TRIALS = 4
LANES = 128
ROWS = 16
MESH = pl.DeviceIdType.MESH
step_scales = (1.0, 0.5, 0.25, 0.125)


def far_first(count):
    return sorted(range(1, count), key=lambda j: -min(j, count - j))


def take_lanes(table, index):
    return jnp.take_along_axis(table, index, axis=1, mode="promise_in_bounds")


def cofactor(m):
    return [
        [
            m[1][1] * m[2][2] - m[1][2] * m[2][1],
            m[1][2] * m[2][0] - m[1][0] * m[2][2],
            m[1][0] * m[2][1] - m[1][1] * m[2][0],
        ],
        [
            m[0][2] * m[2][1] - m[0][1] * m[2][2],
            m[0][0] * m[2][2] - m[0][2] * m[2][0],
            m[0][1] * m[2][0] - m[0][0] * m[2][1],
        ],
        [
            m[0][1] * m[1][2] - m[0][2] * m[1][1],
            m[0][2] * m[1][0] - m[0][0] * m[1][2],
            m[0][0] * m[1][1] - m[0][1] * m[1][0],
        ],
    ]


def split3(x):
    high = x.astype(jnp.bfloat16)
    rest = x - high.astype(jnp.float32)
    mid = rest.astype(jnp.bfloat16)
    low = (rest - mid.astype(jnp.float32)).astype(jnp.bfloat16)
    return jnp.concatenate([high, mid, low], axis=0)


def dot_nt(a, b):
    return lax.dot_general(a, b, (((1,), (1,)), ((), ())), preferred_element_type=jnp.float32)


def fold3(acc):
    return acc[:ROWS] + acc[ROWS : 2 * ROWS] + acc[2 * ROWS :]


def pack(values, op):
    lane = lax.broadcasted_iota(jnp.int32, (8, LANES), 1)
    half = [op(v, pltpu.roll(v, 64, 1)) for v in values]
    first = jnp.where(lane < 64, half[0], half[1])
    second = jnp.where(lane < 64, half[2], half[3])
    first = op(first, pltpu.roll(first, 32, 1))
    second = op(second, pltpu.roll(second, 96, 1))
    return jnp.where((lane // 32) % 2 == 1, first, second)


def unpack_mask():
    lane = lax.broadcasted_iota(jnp.int32, (8, LANES), 1)
    row = lax.broadcasted_iota(jnp.int32, (8, LANES), 0)
    group = lane // 32
    trial = jnp.where(group == 0, 2, jnp.where(group == 1, 0, jnp.where(group == 2, 3, 1)))
    return trial == row


def kernel(
    nd,
    ns,
    coords,
    direction,
    connect,
    shape_inv,
    weight,
    send_node,
    recv_slot,
    grad_ref,
    stat_ref,
    co_v,
    di_v,
    con_v,
    inv_v,
    w_v,
    snd_v,
    rcv_v,
    out_tile,
    halo,
    idx_v,
    onehot,
    back_hot,
    cmat,
    gtile,
    gback,
    rows_v,
    sub_min,
    dom_min,
    sub_sum,
    dom_sum,
    in_sem,
    halo_send,
    halo_recv,
    back_send,
    back_recv,
    sub_sems,
    dom_sems,
):
    f32 = jnp.float32
    d = lax.axis_index("dom")
    s = lax.axis_index("sub")
    nodes = co_v.shape[1]
    local = onehot.shape[0]
    chunks = con_v.shape[0] * 8

    loads = [
        pltpu.make_async_copy(coords, co_v, in_sem.at[0]),
        pltpu.make_async_copy(direction, di_v, in_sem.at[1]),
        pltpu.make_async_copy(send_node, snd_v, in_sem.at[2]),
        pltpu.make_async_copy(recv_slot, rcv_v, in_sem.at[3]),
        pltpu.make_async_copy(weight, w_v, in_sem.at[4]),
    ]
    wide = []
    for k in range(8):
        cut = pl.ds(k * LANES, LANES)
        wide.append(pltpu.make_async_copy(connect.at[:, cut], con_v.at[:, k, :], in_sem.at[5 + k]))
        wide.append(pltpu.make_async_copy(shape_inv.at[:, cut], inv_v.at[:, k, :], in_sem.at[13 + k]))
    for copy in loads + wide:
        copy.start()

    barrier = pltpu.get_barrier_semaphore()
    for j in far_first(ns):
        pl.semaphore_signal(barrier, inc=1, device_id=(d, lax.rem(s + j, ns)), device_id_type=MESH)
    for j in far_first(nd):
        pl.semaphore_signal(barrier, inc=1, device_id=(lax.rem(d + j, nd), s), device_id_type=MESH)

    lane = lax.broadcasted_iota(jnp.int32, (8, LANES), 1)
    block = lane // 32
    for copy in loads:
        copy.wait()

    send_idx = jnp.broadcast_to(snd_v[...], (8, LANES))
    pad = jnp.zeros((2, nodes), f32)
    both = jnp.concatenate([co_v[...], di_v[...], pad], axis=0)
    picked = take_lanes(both[:, :LANES], send_idx & 127)
    for k in range(1, nodes // LANES):
        part = take_lanes(both[:, k * LANES : (k + 1) * LANES], send_idx & 127)
        picked = jnp.where(send_idx >= k * LANES, part, picked)
    out_tile[...] = picked

    pl.semaphore_wait(barrier, nd - 1 + ns - 1)

    ahead = (
        (lax.rem(d + 1, nd), s),
        (lax.rem(d + nd - 1, nd), s),
        (d, lax.rem(s + 1, ns)),
        (d, lax.rem(s + ns - 1, ns)),
    )
    behind = (ahead[1], ahead[0], ahead[3], ahead[2])
    shares = [
        pltpu.make_async_remote_copy(
            src_ref=out_tile,
            dst_ref=halo.at[k],
            send_sem=halo_send.at[k],
            recv_sem=halo_recv.at[k],
            device_id=ahead[k],
            device_id_type=MESH,
        )
        for k in range(4)
    ]
    for copy in shares:
        copy.start()

    for copy in wide:
        copy.wait()

    slot_row = jnp.broadcast_to(rcv_v[...], (LANES, LANES))
    slot_hot = jnp.where(slot_row == lax.broadcasted_iota(jnp.int32, (LANES, LANES), 0), 1.0, 0.0).astype(jnp.bfloat16)
    arrival = dot_nt(lane.astype(f32).astype(jnp.bfloat16), slot_hot).astype(jnp.int32)
    corner = []
    for c in range(4):
        idx = con_v[c]
        ghost = idx >= nodes
        idx = jnp.where(ghost, nodes + take_lanes(arrival, jnp.where(ghost, idx - nodes, 0)), idx)
        idx_v[pl.ds(8 * c, 8), :] = idx
        corner.append(idx)

    owned = []
    for q in range(6):
        source = (co_v if q < 3 else di_v)
        r = q % 3
        per = []
        for c in range(4):
            low = corner[c] & 127
            value = take_lanes(jnp.broadcast_to(source[r : r + 1, :LANES], (8, LANES)), low)
            for k in range(1, nodes // LANES):
                part = take_lanes(
                    jnp.broadcast_to(source[r : r + 1, k * LANES : (k + 1) * LANES], (8, LANES)), low
                )
                value = jnp.where(corner[c] >= k * LANES, part, value)
            per.append(value)
        owned.append(per)

    send_row = jnp.broadcast_to(snd_v[...], (nodes, LANES))
    back_hot[...] = jnp.where(
        send_row == lax.broadcasted_iota(jnp.int32, (nodes, LANES), 0), 1.0, 0.0
    ).astype(jnp.bfloat16)

    for copy in shares:
        copy.wait_recv()
    came = halo[0]
    for k in range(1, 4):
        came = jnp.where(block == k, halo[k], came)

    values = []
    for q in range(6):
        row = jnp.broadcast_to(came[q : q + 1, :], (8, LANES))
        values.append(
            [jnp.where(corner[c] >= nodes, take_lanes(row, corner[c] & 127), owned[q][c]) for c in range(4)]
        )
    w9 = [inv_v[i] for i in range(9)]

    def edges_times_inverse(base):
        out = []
        for r in range(3):
            edge = [values[base + r][c] - values[base + r][0] for c in (1, 2, 3)]
            out.append([edge[0] * w9[m] + edge[1] * w9[3 + m] + edge[2] * w9[6 + m] for m in range(3)])
        return out

    jac_x = edges_times_inverse(0)
    jac_d = edges_times_inverse(3)
    jacs = []
    cofs = []
    dets = []
    for t in range(TRIALS):
        a = step_scales[t]
        m = [[jac_x[r][k] + a * jac_d[r][k] for k in range(3)] for r in range(3)]
        cof = cofactor(m)
        jacs.append(m)
        cofs.append(cof)
        dets.append(m[0][0] * cof[0][0] + m[0][1] * cof[0][1] + m[0][2] * cof[0][2])

    def start_stage(row, buf, sems, axis):
        me, count = (s, ns) if axis == "sub" else (d, nd)
        copies = []
        for j in far_first(count):
            peer = lax.rem(me + j, count)
            copies.append(
                pltpu.make_async_remote_copy(
                    src_ref=row,
                    dst_ref=buf.at[pl.ds(me, 1), :],
                    send_sem=sems.at[0, j - 1],
                    recv_sem=sems.at[1, j - 1],
                    device_id=(d, peer) if axis == "sub" else (peer, s),
                    device_id_type=MESH,
                )
            )
        for copy in copies:
            copy.start()
        return copies

    def finish_stage(row, buf, copies, axis, reduce):
        me, count = (s, ns) if axis == "sub" else (d, nd)
        for copy in copies:
            copy.wait_recv()
        mine = lax.broadcasted_iota(jnp.int32, (count, LANES), 0) == me
        return reduce(jnp.where(mine, row, buf[...]), axis=0, keepdims=True)

    def build_hot(first, last):
        node = lax.broadcasted_iota(jnp.int32, (local, LANES), 0)

        def step(j, carry):
            row = jnp.broadcast_to(idx_v[pl.ds(j, 1), :], (local, LANES))
            onehot[:, pl.ds(pl.multiple_of(j * LANES, LANES), LANES)] = jnp.where(row == node, 1.0, 0.0).astype(
                jnp.bfloat16
            )
            return carry

        lax.fori_loop(first, last, step, 0)

    row = jnp.min(pack(dets, jnp.minimum), axis=0, keepdims=True)
    rows_v[0] = row
    flights = start_stage(rows_v.at[0], sub_min, sub_sems.at[0], "sub")
    sends = list(flights)
    weights = w_v[...]
    squares = []
    for t in range(TRIALS):
        total = jacs[t][0][0] * jacs[t][0][0]
        for r in range(3):
            for k in range(3):
                if r + k > 0:
                    total = total + jacs[t][r][k] * jacs[t][r][k]
        squares.append(weights * total)
    build_hot(0, chunks // 2)
    row = finish_stage(row, sub_min, flights, "sub", jnp.min)
    rows_v[1] = row
    flights = start_stage(rows_v.at[1], dom_min, dom_sems.at[0], "dom")
    sends += flights
    build_hot(chunks // 2, chunks)
    row = finish_stage(row, dom_min, flights, "dom", jnp.min)

    mask = unpack_mask()
    lowest = jnp.min(jnp.where(mask, jnp.broadcast_to(row, (8, LANES)), jnp.inf), axis=1, keepdims=True)
    shift = lowest - 1.0 - jnp.abs(lowest)

    energies = []
    scale_jac = []
    scale_cof = []
    for t in range(TRIALS):
        lifted = dets[t] - jnp.broadcast_to(shift[t : t + 1, :], (8, LANES))
        power = jnp.exp(jnp.log(lifted) * (-2.0 / 3.0))
        energy = squares[t] * power
        energies.append(energy)
        scale_jac.append(weights * power * (2.0 / 3.0))
        scale_cof.append(energy / lifted * (2.0 / 9.0))

    row = jnp.sum(pack(energies, jnp.add), axis=0, keepdims=True)
    rows_v[2] = row
    flights = start_stage(rows_v.at[2], sub_sum, sub_sems.at[1], "sub")
    sends += flights

    for t in range(TRIALS):
        for r in range(3):
            g = [scale_jac[t] * jacs[t][r][k] - scale_cof[t] * cofs[t][r][k] for k in range(3)]
            h = [g[0] * w9[3 * e] + g[1] * w9[3 * e + 1] + g[2] * w9[3 * e + 2] for e in range(3)]
            h = [-(h[0] + h[1] + h[2])] + h
            for c in range(4):
                cmat[pl.ds(8 * ROWS * c + 3 * t + r, 8, stride=ROWS), :] = h[c]

    def scatter_step(j, acc):
        pair = [split3(cmat[pl.ds(pl.multiple_of((2 * j + i) * ROWS, ROWS), ROWS), :]) for i in range(2)]
        left = jnp.concatenate(pair, axis=1)
        right = onehot[:, pl.ds(pl.multiple_of(j * 2 * LANES, LANES), 2 * LANES)]
        return acc + dot_nt(left, right)

    summed = fold3(lax.fori_loop(0, chunks // 2, scatter_step, jnp.zeros((3 * ROWS, local), f32)))
    gtile[...] = summed[:, nodes:]
    returns = [
        pltpu.make_async_remote_copy(
            src_ref=gtile,
            dst_ref=gback.at[k],
            send_sem=back_send.at[k],
            recv_sem=back_recv.at[k],
            device_id=behind[k],
            device_id_type=MESH,
        )
        for k in range(4)
    ]
    for copy in returns:
        copy.start()

    row = finish_stage(row, sub_sum, flights, "sub", jnp.sum)
    rows_v[3] = row
    flights = start_stage(rows_v.at[3], dom_sum, dom_sems.at[1], "dom")
    sends += flights

    for copy in returns:
        copy.wait_recv()
    wide_block = lax.broadcasted_iota(jnp.int32, (ROWS, LANES), 1) // 32
    came = gback[0]
    for k in range(1, 4):
        came = jnp.where(wide_block == k, gback[k], came)
    total = summed[:, :nodes] + fold3(dot_nt(split3(came), back_hot[...]))
    for t in range(TRIALS):
        grad_ref[t] = total[3 * t : 3 * t + 3, :]

    row = finish_stage(row, dom_sum, flights, "dom", jnp.sum)
    energy = jnp.sum(jnp.where(mask, jnp.broadcast_to(row, (8, LANES)), 0.0), axis=1, keepdims=True)
    energy = energy / 3.0 / (nd * ns * chunks // 4 * LANES)
    diagonal = lane == lax.broadcasted_iota(jnp.int32, (8, LANES), 0)
    stat_ref[0:1, :] = jnp.sum(jnp.where(diagonal, energy, 0.0), axis=0, keepdims=True)
    stat_ref[1:2, :] = jnp.sum(jnp.where(diagonal, jnp.where(lowest < jnp.inf, lowest, 0.0), 0.0), axis=0, keepdims=True)

    for copy in shares + sends + returns:
        copy.wait_send()


def per_device(nd, ns, coords, direction, connect, shape_inv, weight, send_node, recv_slot):
    f32 = jnp.float32
    nodes = coords.shape[1]
    ghosts = send_node.shape[1]
    local = nodes + ghosts
    elems = connect.shape[1]
    per_row = elems // LANES
    chunks = 4 * per_row
    dma = pltpu.SemaphoreType.DMA
    any_space = pl.BlockSpec(memory_space=pl.ANY)
    vmem = pl.BlockSpec(memory_space=pltpu.VMEM)
    gradient, stats = pl.pallas_call(
        functools.partial(kernel, nd, ns),
        out_shape=(
            jax.ShapeDtypeStruct((TRIALS, 3, nodes), f32),
            jax.ShapeDtypeStruct((2, LANES), f32),
        ),
        in_specs=[any_space] * 7,
        out_specs=(vmem, vmem),
        scratch_shapes=[
            pltpu.VMEM((3, nodes), f32),
            pltpu.VMEM((3, nodes), f32),
            pltpu.VMEM((4, per_row, LANES), jnp.int32),
            pltpu.VMEM((9, per_row, LANES), f32),
            pltpu.VMEM((per_row, LANES), f32),
            pltpu.VMEM((1, ghosts), jnp.int32),
            pltpu.VMEM((1, ghosts), jnp.int32),
            pltpu.VMEM((8, ghosts), f32),
            pltpu.VMEM((4, 8, ghosts), f32),
            pltpu.VMEM((chunks, LANES), jnp.int32),
            pltpu.VMEM((local, 4 * elems), jnp.bfloat16),
            pltpu.VMEM((nodes, ghosts), jnp.bfloat16),
            pltpu.VMEM((chunks * ROWS, LANES), f32),
            pltpu.VMEM((ROWS, ghosts), f32),
            pltpu.VMEM((4, ROWS, ghosts), f32),
            pltpu.VMEM((4, 1, LANES), f32),
            pltpu.VMEM((ns, LANES), f32),
            pltpu.VMEM((nd, LANES), f32),
            pltpu.VMEM((ns, LANES), f32),
            pltpu.VMEM((nd, LANES), f32),
            dma((21,)),
            dma((4,)),
            dma((4,)),
            dma((4,)),
            dma((4,)),
            dma((2, 2, ns - 1)),
            dma((2, 2, nd - 1)),
        ],
        compiler_params=pltpu.CompilerParams(collective_id=0, has_side_effects=True),
        name="trial_energy",
    )(coords, direction, connect, shape_inv, weight.reshape(per_row, LANES), send_node, recv_slot)
    return gradient, stats[0, :TRIALS], stats[1, :TRIALS]


def solution(mesh):
    placed = (
        P(None, ("dom", "sub")),
        P(None, ("dom", "sub")),
        P(None, ("dom", "sub")),
        P(None, ("dom", "sub")),
        P(("dom", "sub")),
        P(("dom", "sub"), None),
        P(("dom", "sub"), None),
    )
    return jax.shard_map(
        functools.partial(per_device, mesh.shape["dom"], mesh.shape["sub"]),
        mesh=mesh,
        in_specs=placed,
        out_specs=(P(None, None, ("dom", "sub")), P(), P()),
        check_vma=False,
    )
```

```python
import functools

import jax
import jax.numpy as jnp
from jax import lax
from jax.experimental import pallas as pl
from jax.experimental.pallas import tpu as pltpu
from jax.sharding import PartitionSpec as P

TRIALS = 4
LANES = 128
ROWS = 16
MESH = pl.DeviceIdType.MESH
step_scales = (1.0, 0.5, 0.25, 0.125)


def far_first(count, width=1):
    def far(j):
        x, y = j % width, j // width
        return min(x, width - x) + min(y, count // width - y)

    return sorted(range(1, count), key=lambda j: -far(j))


def take_lanes(table, index):
    return jnp.take_along_axis(table, index, axis=1, mode="promise_in_bounds")


def cofactor(m):
    return [
        [
            m[1][1] * m[2][2] - m[1][2] * m[2][1],
            m[1][2] * m[2][0] - m[1][0] * m[2][2],
            m[1][0] * m[2][1] - m[1][1] * m[2][0],
        ],
        [
            m[0][2] * m[2][1] - m[0][1] * m[2][2],
            m[0][0] * m[2][2] - m[0][2] * m[2][0],
            m[0][1] * m[2][0] - m[0][0] * m[2][1],
        ],
        [
            m[0][1] * m[1][2] - m[0][2] * m[1][1],
            m[0][2] * m[1][0] - m[0][0] * m[1][2],
            m[0][0] * m[1][1] - m[0][1] * m[1][0],
        ],
    ]


def split3(x):
    high = x.astype(jnp.bfloat16)
    rest = x - high.astype(jnp.float32)
    mid = rest.astype(jnp.bfloat16)
    low = (rest - mid.astype(jnp.float32)).astype(jnp.bfloat16)
    return jnp.concatenate([high, mid, low], axis=0)


def dot_nt(a, b):
    return lax.dot_general(a, b, (((1,), (1,)), ((), ())), preferred_element_type=jnp.float32)


def fold3(acc):
    return acc[:ROWS] + acc[ROWS : 2 * ROWS] + acc[2 * ROWS :]


def pack(values, op):
    lane = lax.broadcasted_iota(jnp.int32, (8, LANES), 1)
    half = [op(v, pltpu.roll(v, 64, 1)) for v in values]
    first = jnp.where(lane < 64, half[0], half[1])
    second = jnp.where(lane < 64, half[2], half[3])
    first = op(first, pltpu.roll(first, 32, 1))
    second = op(second, pltpu.roll(second, 96, 1))
    return jnp.where((lane // 32) % 2 == 1, first, second)


def unpack_mask():
    lane = lax.broadcasted_iota(jnp.int32, (8, LANES), 1)
    row = lax.broadcasted_iota(jnp.int32, (8, LANES), 0)
    group = lane // 32
    trial = jnp.where(group == 0, 2, jnp.where(group == 1, 0, jnp.where(group == 2, 3, 1)))
    return trial == row


def kernel(
    nd,
    ns,
    coords,
    direction,
    connect,
    shape_inv,
    weight,
    send_node,
    recv_slot,
    grad_ref,
    stat_ref,
    co_v,
    di_v,
    con_v,
    inv_v,
    w_v,
    snd_v,
    rcv_v,
    out_tile,
    halo,
    idx_v,
    onehot,
    back_hot,
    cmat,
    gtile,
    gback,
    rows_v,
    sub_min,
    dom_min,
    sub_sum,
    dom_sum,
    in_sem,
    halo_send,
    halo_recv,
    back_send,
    back_recv,
    sub_sems,
    dom_sems,
    known,
):
    f32 = jnp.float32
    d = lax.axis_index("dom")
    s = lax.axis_index("sub")
    nodes = co_v.shape[1]
    local = onehot.shape[0]
    chunks = con_v.shape[0] * 8

    loads = [
        pltpu.make_async_copy(coords, co_v, in_sem.at[0]),
        pltpu.make_async_copy(direction, di_v, in_sem.at[1]),
        pltpu.make_async_copy(send_node, snd_v, in_sem.at[2]),
        pltpu.make_async_copy(recv_slot, rcv_v, in_sem.at[3]),
        pltpu.make_async_copy(weight, w_v, in_sem.at[4]),
    ]
    wide = []
    for k in range(8):
        cut = pl.ds(k * LANES, LANES)
        wide.append(pltpu.make_async_copy(connect.at[:, cut], con_v.at[:, k, :], in_sem.at[5 + k]))
        wide.append(pltpu.make_async_copy(shape_inv.at[:, cut], inv_v.at[:, k, :], in_sem.at[13 + k]))
    for copy in loads[:3]:
        copy.start()

    barrier = pltpu.get_barrier_semaphore()
    for j in far_first(nd, 4):
        pl.semaphore_signal(barrier, inc=1, device_id=(lax.rem(d + j, nd), s), device_id_type=MESH)
    for j in (1, ns - 1):
        pl.semaphore_signal(barrier, inc=1, device_id=(d, lax.rem(s + j, ns)), device_id_type=MESH)
    for copy in loads[3:] + wide:
        copy.start()

    lane = lax.broadcasted_iota(jnp.int32, (8, LANES), 1)
    block = lane // 32
    for copy in loads[:3]:
        copy.wait()

    send_idx = jnp.broadcast_to(snd_v[...], (8, LANES))
    pad = jnp.zeros((2, nodes), f32)
    both = jnp.concatenate([co_v[...], di_v[...], pad], axis=0)
    picked = take_lanes(both[:, :LANES], send_idx & 127)
    for k in range(1, nodes // LANES):
        part = take_lanes(both[:, k * LANES : (k + 1) * LANES], send_idx & 127)
        picked = jnp.where(send_idx >= k * LANES, part, picked)
    out_tile[...] = picked

    pl.semaphore_wait(barrier, nd - 1 + 2)

    ahead = (
        (lax.rem(d + 1, nd), s),
        (lax.rem(d + nd - 1, nd), s),
        (d, lax.rem(s + 1, ns)),
        (d, lax.rem(s + ns - 1, ns)),
    )
    behind = (ahead[1], ahead[0], ahead[3], ahead[2])
    shares = [
        pltpu.make_async_remote_copy(
            src_ref=out_tile,
            dst_ref=halo.at[k],
            send_sem=halo_send.at[k],
            recv_sem=halo_recv.at[k],
            device_id=ahead[k],
            device_id_type=MESH,
        )
        for k in range(4)
    ]
    for copy in shares:
        copy.start()

    for copy in loads[3:] + wide:
        copy.wait()

    slot_row = jnp.broadcast_to(rcv_v[...], (LANES, LANES))
    slot_hot = jnp.where(slot_row == lax.broadcasted_iota(jnp.int32, (LANES, LANES), 0), 1.0, 0.0).astype(jnp.bfloat16)
    arrival = dot_nt(lane.astype(f32).astype(jnp.bfloat16), slot_hot).astype(jnp.int32)
    corner = []
    for c in range(4):
        idx = con_v[c]
        ghost = idx >= nodes
        idx = jnp.where(ghost, nodes + take_lanes(arrival, jnp.where(ghost, idx - nodes, 0)), idx)
        idx_v[pl.ds(8 * c, 8), :] = idx
        corner.append(idx)

    owned = []
    for q in range(6):
        source = (co_v if q < 3 else di_v)
        r = q % 3
        per = []
        for c in range(4):
            low = corner[c] & 127
            value = take_lanes(jnp.broadcast_to(source[r : r + 1, :LANES], (8, LANES)), low)
            for k in range(1, nodes // LANES):
                part = take_lanes(
                    jnp.broadcast_to(source[r : r + 1, k * LANES : (k + 1) * LANES], (8, LANES)), low
                )
                value = jnp.where(corner[c] >= k * LANES, part, value)
            per.append(value)
        owned.append(per)

    send_row = jnp.broadcast_to(snd_v[...], (nodes, LANES))
    back_hot[...] = jnp.where(
        send_row == lax.broadcasted_iota(jnp.int32, (nodes, LANES), 0), 1.0, 0.0
    ).astype(jnp.bfloat16)

    for copy in shares:
        copy.wait_recv()
    reach = 2
    hops = []
    while reach < ns // 2:
        hops.append(reach)
        reach *= 2

    def greet(i):
        for j in (hops[i], ns - hops[i]):
            pl.semaphore_signal(known.at[i], inc=1, device_id=(d, lax.rem(s + j, ns)), device_id_type=MESH)

    if hops:
        greet(0)
    came = halo[0]
    for k in range(1, 4):
        came = jnp.where(block == k, halo[k], came)

    values = []
    for q in range(6):
        row = jnp.broadcast_to(came[q : q + 1, :], (8, LANES))
        values.append(
            [jnp.where(corner[c] >= nodes, take_lanes(row, corner[c] & 127), owned[q][c]) for c in range(4)]
        )
    w9 = [inv_v[i] for i in range(9)]

    def edges_times_inverse(base):
        out = []
        for r in range(3):
            edge = [values[base + r][c] - values[base + r][0] for c in (1, 2, 3)]
            out.append([edge[0] * w9[m] + edge[1] * w9[3 + m] + edge[2] * w9[6 + m] for m in range(3)])
        return out

    jac_x = edges_times_inverse(0)
    jac_d = edges_times_inverse(3)
    jacs = []
    cofs = []
    dets = []
    for t in range(TRIALS):
        a = step_scales[t]
        m = [[jac_x[r][k] + a * jac_d[r][k] for k in range(3)] for r in range(3)]
        cof = cofactor(m)
        jacs.append(m)
        cofs.append(cof)
        dets.append(m[0][0] * cof[0][0] + m[0][1] * cof[0][1] + m[0][2] * cof[0][2])

    def start_stage(row, buf, sems, axis):
        me, count = (s, ns) if axis == "sub" else (d, nd)
        copies = []
        for j in far_first(count, 1 if axis == "sub" else 4):
            peer = lax.rem(me + j, count)
            copies.append(
                pltpu.make_async_remote_copy(
                    src_ref=row,
                    dst_ref=buf.at[pl.ds(me, 1), :],
                    send_sem=sems.at[0, j - 1],
                    recv_sem=sems.at[1, j - 1],
                    device_id=(d, peer) if axis == "sub" else (peer, s),
                    device_id_type=MESH,
                )
            )
        for copy in copies:
            copy.start()
        return copies

    def finish_stage(row, buf, copies, axis, reduce):
        me, count = (s, ns) if axis == "sub" else (d, nd)
        for copy in copies:
            copy.wait_recv()
        mine = lax.broadcasted_iota(jnp.int32, (count, LANES), 0) == me
        return reduce(jnp.where(mine, row, buf[...]), axis=0, keepdims=True)

    def build_hot(first, last):
        node = lax.broadcasted_iota(jnp.int32, (local, LANES), 0)

        def step(j, carry):
            row = jnp.broadcast_to(idx_v[pl.ds(j, 1), :], (local, LANES))
            onehot[:, pl.ds(pl.multiple_of(j * LANES, LANES), LANES)] = jnp.where(row == node, 1.0, 0.0).astype(
                jnp.bfloat16
            )
            return carry

        lax.fori_loop(first, last, step, 0)

    row = jnp.min(pack(dets, jnp.minimum), axis=0, keepdims=True)
    rows_v[0] = row
    flights = start_stage(rows_v.at[0], dom_min, dom_sems.at[0], "dom")
    sends = list(flights)
    weights = w_v[...]
    squares = []
    for t in range(TRIALS):
        total = jacs[t][0][0] * jacs[t][0][0]
        for r in range(3):
            for k in range(3):
                if r + k > 0:
                    total = total + jacs[t][r][k] * jacs[t][r][k]
        squares.append(weights * total)
    build_hot(0, chunks // 2)
    for i in range(len(hops)):
        pl.semaphore_wait(known.at[i], 2)
        if i + 1 < len(hops):
            greet(i + 1)
    row = finish_stage(row, dom_min, flights, "dom", jnp.min)
    rows_v[1] = row
    flights = start_stage(rows_v.at[1], sub_min, sub_sems.at[0], "sub")
    sends += flights
    build_hot(chunks // 2, chunks)
    row = finish_stage(row, sub_min, flights, "sub", jnp.min)

    mask = unpack_mask()
    lowest = jnp.min(jnp.where(mask, jnp.broadcast_to(row, (8, LANES)), jnp.inf), axis=1, keepdims=True)
    shift = lowest - 1.0 - jnp.abs(lowest)

    energies = []
    scale_jac = []
    scale_cof = []
    for t in range(TRIALS):
        lifted = dets[t] - jnp.broadcast_to(shift[t : t + 1, :], (8, LANES))
        power = jnp.exp(jnp.log(lifted) * (-2.0 / 3.0))
        energy = squares[t] * power
        energies.append(energy)
        scale_jac.append(weights * power * (2.0 / 3.0))
        scale_cof.append(energy / lifted * (2.0 / 9.0))

    row = jnp.sum(pack(energies, jnp.add), axis=0, keepdims=True)
    rows_v[2] = row
    flights = start_stage(rows_v.at[2], sub_sum, sub_sems.at[1], "sub")
    sends += flights

    for t in range(TRIALS):
        for r in range(3):
            g = [scale_jac[t] * jacs[t][r][k] - scale_cof[t] * cofs[t][r][k] for k in range(3)]
            h = [g[0] * w9[3 * e] + g[1] * w9[3 * e + 1] + g[2] * w9[3 * e + 2] for e in range(3)]
            h = [-(h[0] + h[1] + h[2])] + h
            for c in range(4):
                cmat[pl.ds(8 * ROWS * c + TRIALS * r + t, 8, stride=ROWS), :] = h[c]

    def scatter_step(j, acc):
        pair = [split3(cmat[pl.ds(pl.multiple_of((2 * j + i) * ROWS, ROWS), ROWS), :]) for i in range(2)]
        left = jnp.concatenate(pair, axis=1)
        right = onehot[:, pl.ds(pl.multiple_of(j * 2 * LANES, LANES), 2 * LANES)]
        return acc + dot_nt(left, right)

    summed = fold3(lax.fori_loop(0, chunks // 2, scatter_step, jnp.zeros((3 * ROWS, local), f32)))
    gtile[...] = summed[:, nodes:]
    returns = [
        pltpu.make_async_remote_copy(
            src_ref=gtile,
            dst_ref=gback.at[k],
            send_sem=back_send.at[k],
            recv_sem=back_recv.at[k],
            device_id=behind[k],
            device_id_type=MESH,
        )
        for k in range(4)
    ]
    for copy in returns:
        copy.start()

    row = finish_stage(row, sub_sum, flights, "sub", jnp.sum)
    rows_v[3] = row
    flights = start_stage(rows_v.at[3], dom_sum, dom_sems.at[1], "dom")
    sends += flights

    for copy in returns:
        copy.wait_recv()
    wide_block = lax.broadcasted_iota(jnp.int32, (ROWS, LANES), 1) // 32
    came = gback[0]
    for k in range(1, 4):
        came = jnp.where(wide_block == k, gback[k], came)
    total = summed[:, :nodes] + fold3(dot_nt(split3(came), back_hot[...]))
    for r in range(3):
        grad_ref[r] = total[TRIALS * r : TRIALS * r + TRIALS, :]

    row = finish_stage(row, dom_sum, flights, "dom", jnp.sum)
    energy = jnp.sum(jnp.where(mask, jnp.broadcast_to(row, (8, LANES)), 0.0), axis=1, keepdims=True)
    energy = energy / 3.0 / (nd * ns * chunks // 4 * LANES)
    diagonal = lane == lax.broadcasted_iota(jnp.int32, (8, LANES), 0)
    stat_ref[0:1, :] = jnp.sum(jnp.where(diagonal, energy, 0.0), axis=0, keepdims=True)
    stat_ref[1:2, :] = jnp.sum(jnp.where(diagonal, jnp.where(lowest < jnp.inf, lowest, 0.0), 0.0), axis=0, keepdims=True)

    for copy in shares + sends + returns:
        copy.wait_send()


def per_device(nd, ns, coords, direction, connect, shape_inv, weight, send_node, recv_slot):
    f32 = jnp.float32
    nodes = coords.shape[1]
    ghosts = send_node.shape[1]
    local = nodes + ghosts
    elems = connect.shape[1]
    per_row = elems // LANES
    chunks = 4 * per_row
    dma = pltpu.SemaphoreType.DMA
    any_space = pl.BlockSpec(memory_space=pl.ANY)
    vmem = pl.BlockSpec(memory_space=pltpu.VMEM)
    operands = (coords, direction, connect, shape_inv, weight.reshape(per_row, LANES), send_node, recv_slot)
    gradient, stats = pl.pallas_call(
        functools.partial(kernel, nd, ns),
        out_shape=(
            jax.ShapeDtypeStruct((3, TRIALS, nodes), f32),
            jax.ShapeDtypeStruct((2, LANES), f32),
        ),
        in_specs=[any_space] * 7,
        out_specs=(vmem, vmem),
        scratch_shapes=[
            pltpu.VMEM((3, nodes), f32),
            pltpu.VMEM((3, nodes), f32),
            pltpu.VMEM((4, per_row, LANES), jnp.int32),
            pltpu.VMEM((9, per_row, LANES), f32),
            pltpu.VMEM((per_row, LANES), f32),
            pltpu.VMEM((1, ghosts), jnp.int32),
            pltpu.VMEM((1, ghosts), jnp.int32),
            pltpu.VMEM((8, ghosts), f32),
            pltpu.VMEM((4, 8, ghosts), f32),
            pltpu.VMEM((chunks, LANES), jnp.int32),
            pltpu.VMEM((local, 4 * elems), jnp.bfloat16),
            pltpu.VMEM((nodes, ghosts), jnp.bfloat16),
            pltpu.VMEM((chunks * ROWS, LANES), f32),
            pltpu.VMEM((ROWS, ghosts), f32),
            pltpu.VMEM((4, ROWS, ghosts), f32),
            pltpu.VMEM((4, 1, LANES), f32),
            pltpu.VMEM((ns, LANES), f32),
            pltpu.VMEM((nd, LANES), f32),
            pltpu.VMEM((ns, LANES), f32),
            pltpu.VMEM((nd, LANES), f32),
            dma((21,)),
            dma((4,)),
            dma((4,)),
            dma((4,)),
            dma((4,)),
            dma((2, 2, ns - 1)),
            dma((2, 2, nd - 1)),
            pltpu.SemaphoreType.REGULAR((4,)),
        ],
        compiler_params=pltpu.CompilerParams(
            collective_id=0, has_side_effects=True, vmem_limit_bytes=1 << 24
        ),
        name="trial_energy",
    )(*(pltpu.with_memory_space_constraint(x, pltpu.HBM) for x in operands))
    return gradient.transpose(1, 0, 2), stats[0, :TRIALS], stats[1, :TRIALS]


def solution(mesh):
    placed = (
        P(None, ("dom", "sub")),
        P(None, ("dom", "sub")),
        P(None, ("dom", "sub")),
        P(None, ("dom", "sub")),
        P(("dom", "sub")),
        P(("dom", "sub"), None),
        P(("dom", "sub"), None),
    )
    return jax.shard_map(
        functools.partial(per_device, mesh.shape["dom"], mesh.shape["sub"]),
        mesh=mesh,
        in_specs=placed,
        out_specs=(P(None, None, ("dom", "sub")), P(), P()),
        check_vma=False,
    )
```

```python
import functools

import jax
import jax.numpy as jnp
from jax import lax
from jax.experimental import pallas as pl
from jax.experimental.pallas import tpu as pltpu
from jax.sharding import PartitionSpec as P

TRIALS = 4
LANES = 128
ROWS = 16
MESH = pl.DeviceIdType.MESH
step_scales = (1.0, 0.5, 0.25, 0.125)


def far_first(count, width=1):
    def far(j):
        x, y = j % width, j // width
        return min(x, width - x) + min(y, count // width - y)

    return sorted(range(1, count), key=lambda j: -far(j))


def take_lanes(table, index):
    return jnp.take_along_axis(table, index, axis=1, mode="promise_in_bounds")


def cofactor(m):
    return [
        [
            m[1][1] * m[2][2] - m[1][2] * m[2][1],
            m[1][2] * m[2][0] - m[1][0] * m[2][2],
            m[1][0] * m[2][1] - m[1][1] * m[2][0],
        ],
        [
            m[0][2] * m[2][1] - m[0][1] * m[2][2],
            m[0][0] * m[2][2] - m[0][2] * m[2][0],
            m[0][1] * m[2][0] - m[0][0] * m[2][1],
        ],
        [
            m[0][1] * m[1][2] - m[0][2] * m[1][1],
            m[0][2] * m[1][0] - m[0][0] * m[1][2],
            m[0][0] * m[1][1] - m[0][1] * m[1][0],
        ],
    ]


def split3(x):
    high = x.astype(jnp.bfloat16)
    rest = x - high.astype(jnp.float32)
    mid = rest.astype(jnp.bfloat16)
    low = (rest - mid.astype(jnp.float32)).astype(jnp.bfloat16)
    return jnp.concatenate([high, mid, low], axis=0)


def dot_nt(a, b):
    return lax.dot_general(a, b, (((1,), (1,)), ((), ())), preferred_element_type=jnp.float32)


def fold3(acc):
    return acc[:ROWS] + acc[ROWS : 2 * ROWS] + acc[2 * ROWS :]


def pack(values, op):
    lane = lax.broadcasted_iota(jnp.int32, (8, LANES), 1)
    half = [op(v, pltpu.roll(v, 64, 1)) for v in values]
    first = jnp.where(lane < 64, half[0], half[1])
    second = jnp.where(lane < 64, half[2], half[3])
    first = op(first, pltpu.roll(first, 32, 1))
    second = op(second, pltpu.roll(second, 96, 1))
    return jnp.where((lane // 32) % 2 == 1, first, second)


def unpack_mask():
    lane = lax.broadcasted_iota(jnp.int32, (8, LANES), 1)
    row = lax.broadcasted_iota(jnp.int32, (8, LANES), 0)
    group = lane // 32
    trial = jnp.where(group == 0, 2, jnp.where(group == 1, 0, jnp.where(group == 2, 3, 1)))
    return trial == row


def kernel(
    nd,
    ns,
    coords,
    direction,
    connect,
    shape_inv,
    weight,
    send_node,
    recv_slot,
    grad_ref,
    energy_ref,
    lowest_ref,
    co_v,
    di_v,
    con_v,
    inv_v,
    w_v,
    snd_v,
    rcv_v,
    out_tile,
    halo,
    idx_v,
    onehot,
    back_hot,
    cmat,
    gtile,
    gback,
    rows_v,
    sub_min,
    dom_min,
    sub_sum,
    dom_sum,
    in_sem,
    halo_send,
    halo_recv,
    back_send,
    back_recv,
    sub_sems,
    dom_sems,
    known,
):
    f32 = jnp.float32
    d = lax.axis_index("dom")
    s = lax.axis_index("sub")
    nodes = co_v.shape[1]
    local = onehot.shape[0]
    chunks = con_v.shape[0] * 8

    loads = [
        pltpu.make_async_copy(coords, co_v, in_sem.at[0]),
        pltpu.make_async_copy(direction, di_v, in_sem.at[1]),
        pltpu.make_async_copy(send_node, snd_v, in_sem.at[2]),
        pltpu.make_async_copy(recv_slot, rcv_v, in_sem.at[3]),
        pltpu.make_async_copy(weight, w_v, in_sem.at[4]),
    ]
    wide = []
    for k in range(8):
        cut = pl.ds(k * LANES, LANES)
        wide.append(pltpu.make_async_copy(connect.at[:, cut], con_v.at[:, k, :], in_sem.at[5 + k]))
        wide.append(pltpu.make_async_copy(shape_inv.at[:, cut], inv_v.at[:, k, :], in_sem.at[13 + k]))
    for copy in loads[:3]:
        copy.start()

    barrier = pltpu.get_barrier_semaphore()
    for j in far_first(nd, 4):
        pl.semaphore_signal(barrier, inc=1, device_id=(lax.rem(d + j, nd), s), device_id_type=MESH)
    for j in (1, ns - 1):
        pl.semaphore_signal(barrier, inc=1, device_id=(d, lax.rem(s + j, ns)), device_id_type=MESH)
    for copy in loads[3:] + wide:
        copy.start()

    lane = lax.broadcasted_iota(jnp.int32, (8, LANES), 1)
    block = lane // 32
    for copy in loads[:3]:
        copy.wait()

    send_idx = jnp.broadcast_to(snd_v[...], (8, LANES))
    pad = jnp.zeros((2, nodes), f32)
    both = jnp.concatenate([co_v[...], di_v[...], pad], axis=0)
    picked = take_lanes(both[:, :LANES], send_idx & 127)
    for k in range(1, nodes // LANES):
        part = take_lanes(both[:, k * LANES : (k + 1) * LANES], send_idx & 127)
        picked = jnp.where(send_idx >= k * LANES, part, picked)
    out_tile[...] = picked

    pl.semaphore_wait(barrier, nd - 1 + 2)

    ahead = (
        (lax.rem(d + 1, nd), s),
        (lax.rem(d + nd - 1, nd), s),
        (d, lax.rem(s + 1, ns)),
        (d, lax.rem(s + ns - 1, ns)),
    )
    behind = (ahead[1], ahead[0], ahead[3], ahead[2])
    shares = [
        pltpu.make_async_remote_copy(
            src_ref=out_tile,
            dst_ref=halo.at[k],
            send_sem=halo_send.at[k],
            recv_sem=halo_recv.at[k],
            device_id=ahead[k],
            device_id_type=MESH,
        )
        for k in range(4)
    ]
    for copy in shares:
        copy.start()

    for copy in loads[3:] + wide:
        copy.wait()

    slot_row = jnp.broadcast_to(rcv_v[...], (LANES, LANES))
    slot_hot = jnp.where(slot_row == lax.broadcasted_iota(jnp.int32, (LANES, LANES), 0), 1.0, 0.0).astype(jnp.bfloat16)
    arrival = dot_nt(lane.astype(f32).astype(jnp.bfloat16), slot_hot).astype(jnp.int32)
    corner = []
    for c in range(4):
        idx = con_v[c]
        ghost = idx >= nodes
        idx = jnp.where(ghost, nodes + take_lanes(arrival, jnp.where(ghost, idx - nodes, 0)), idx)
        idx_v[pl.ds(8 * c, 8), :] = idx
        corner.append(idx)

    owned = []
    for q in range(6):
        source = (co_v if q < 3 else di_v)
        r = q % 3
        per = []
        for c in range(4):
            low = corner[c] & 127
            value = take_lanes(jnp.broadcast_to(source[r : r + 1, :LANES], (8, LANES)), low)
            for k in range(1, nodes // LANES):
                part = take_lanes(
                    jnp.broadcast_to(source[r : r + 1, k * LANES : (k + 1) * LANES], (8, LANES)), low
                )
                value = jnp.where(corner[c] >= k * LANES, part, value)
            per.append(value)
        owned.append(per)

    send_row = jnp.broadcast_to(snd_v[...], (nodes, LANES))
    back_hot[...] = jnp.where(
        send_row == lax.broadcasted_iota(jnp.int32, (nodes, LANES), 0), 1.0, 0.0
    ).astype(jnp.bfloat16)

    for copy in shares:
        copy.wait_recv()
    reach = 2
    hops = []
    while reach < ns // 2:
        hops.append(reach)
        reach *= 2

    def greet(i):
        for j in (hops[i], ns - hops[i]):
            pl.semaphore_signal(known.at[i], inc=1, device_id=(d, lax.rem(s + j, ns)), device_id_type=MESH)

    if hops:
        greet(0)
    came = halo[0]
    for k in range(1, 4):
        came = jnp.where(block == k, halo[k], came)

    values = []
    for q in range(6):
        row = jnp.broadcast_to(came[q : q + 1, :], (8, LANES))
        values.append(
            [jnp.where(corner[c] >= nodes, take_lanes(row, corner[c] & 127), owned[q][c]) for c in range(4)]
        )
    w9 = [inv_v[i] for i in range(9)]

    def edges_times_inverse(base):
        out = []
        for r in range(3):
            edge = [values[base + r][c] - values[base + r][0] for c in (1, 2, 3)]
            out.append([edge[0] * w9[m] + edge[1] * w9[3 + m] + edge[2] * w9[6 + m] for m in range(3)])
        return out

    jac_x = edges_times_inverse(0)
    jac_d = edges_times_inverse(3)
    jacs = []
    cofs = []
    dets = []
    for t in range(TRIALS):
        a = step_scales[t]
        m = [[jac_x[r][k] + a * jac_d[r][k] for k in range(3)] for r in range(3)]
        cof = cofactor(m)
        jacs.append(m)
        cofs.append(cof)
        dets.append(m[0][0] * cof[0][0] + m[0][1] * cof[0][1] + m[0][2] * cof[0][2])

    def start_stage(row, buf, sems, axis):
        me, count = (s, ns) if axis == "sub" else (d, nd)
        copies = []
        for j in far_first(count, 1 if axis == "sub" else 4):
            peer = lax.rem(me + j, count)
            copies.append(
                pltpu.make_async_remote_copy(
                    src_ref=row,
                    dst_ref=buf.at[pl.ds(me, 1), :],
                    send_sem=sems.at[0, j - 1],
                    recv_sem=sems.at[1, j - 1],
                    device_id=(d, peer) if axis == "sub" else (peer, s),
                    device_id_type=MESH,
                )
            )
        for copy in copies:
            copy.start()
        return copies

    def finish_stage(row, buf, copies, axis, reduce):
        me, count = (s, ns) if axis == "sub" else (d, nd)
        for copy in copies:
            copy.wait_recv()
        mine = lax.broadcasted_iota(jnp.int32, (count, LANES), 0) == me
        return reduce(jnp.where(mine, row, buf[...]), axis=0, keepdims=True)

    def build_hot(first, last):
        node = lax.broadcasted_iota(jnp.int32, (local, LANES), 0)

        def step(j, carry):
            row = jnp.broadcast_to(idx_v[pl.ds(j, 1), :], (local, LANES))
            onehot[:, pl.ds(pl.multiple_of(j * LANES, LANES), LANES)] = jnp.where(row == node, 1.0, 0.0).astype(
                jnp.bfloat16
            )
            return carry

        lax.fori_loop(first, last, step, 0)

    row = jnp.min(pack(dets, jnp.minimum), axis=0, keepdims=True)
    rows_v[0] = row
    flights = start_stage(rows_v.at[0], dom_min, dom_sems.at[0], "dom")
    sends = list(flights)
    weights = w_v[...]
    squares = []
    for t in range(TRIALS):
        total = jacs[t][0][0] * jacs[t][0][0]
        for r in range(3):
            for k in range(3):
                if r + k > 0:
                    total = total + jacs[t][r][k] * jacs[t][r][k]
        squares.append(weights * total)
    build_hot(0, chunks // 2)
    for i in range(len(hops)):
        pl.semaphore_wait(known.at[i], 2)
        if i + 1 < len(hops):
            greet(i + 1)
    row = finish_stage(row, dom_min, flights, "dom", jnp.min)
    rows_v[1] = row
    flights = start_stage(rows_v.at[1], sub_min, sub_sems.at[0], "sub")
    sends += flights
    build_hot(chunks // 2, chunks)
    row = finish_stage(row, sub_min, flights, "sub", jnp.min)

    mask = unpack_mask()
    lowest = jnp.min(jnp.where(mask, jnp.broadcast_to(row, (8, LANES)), jnp.inf), axis=1, keepdims=True)
    shift = lowest - 1.0 - jnp.abs(lowest)

    energies = []
    scale_jac = []
    scale_cof = []
    for t in range(TRIALS):
        lifted = dets[t] - jnp.broadcast_to(shift[t : t + 1, :], (8, LANES))
        power = jnp.exp(jnp.log(lifted) * (-2.0 / 3.0))
        energy = squares[t] * power
        energies.append(energy)
        scale_jac.append(weights * power * (2.0 / 3.0))
        scale_cof.append(energy / lifted * (2.0 / 9.0))

    row = jnp.sum(pack(energies, jnp.add), axis=0, keepdims=True)
    rows_v[2] = row
    flights = start_stage(rows_v.at[2], sub_sum, sub_sems.at[1], "sub")
    sends += flights

    for t in range(TRIALS):
        for r in range(3):
            g = [scale_jac[t] * jacs[t][r][k] - scale_cof[t] * cofs[t][r][k] for k in range(3)]
            h = [g[0] * w9[3 * e] + g[1] * w9[3 * e + 1] + g[2] * w9[3 * e + 2] for e in range(3)]
            h = [-(h[0] + h[1] + h[2])] + h
            for c in range(4):
                cmat[pl.ds(8 * ROWS * c + TRIALS * r + t, 8, stride=ROWS), :] = h[c]

    def scatter_step(j, acc):
        pair = [split3(cmat[pl.ds(pl.multiple_of((2 * j + i) * ROWS, ROWS), ROWS), :]) for i in range(2)]
        left = jnp.concatenate(pair, axis=1)
        right = onehot[:, pl.ds(pl.multiple_of(j * 2 * LANES, LANES), 2 * LANES)]
        return acc + dot_nt(left, right)

    summed = fold3(lax.fori_loop(0, chunks // 2, scatter_step, jnp.zeros((3 * ROWS, local), f32)))
    gtile[...] = summed[:, nodes:]
    returns = [
        pltpu.make_async_remote_copy(
            src_ref=gtile,
            dst_ref=gback.at[k],
            send_sem=back_send.at[k],
            recv_sem=back_recv.at[k],
            device_id=behind[k],
            device_id_type=MESH,
        )
        for k in range(4)
    ]
    for copy in returns:
        copy.start()

    row = finish_stage(row, sub_sum, flights, "sub", jnp.sum)
    rows_v[3] = row
    flights = start_stage(rows_v.at[3], dom_sum, dom_sems.at[1], "dom")
    sends += flights

    for copy in returns:
        copy.wait_recv()
    wide_block = lax.broadcasted_iota(jnp.int32, (ROWS, LANES), 1) // 32
    came = gback[0]
    for k in range(1, 4):
        came = jnp.where(wide_block == k, gback[k], came)
    total = summed[:, :nodes] + fold3(dot_nt(split3(came), back_hot[...]))
    for r in range(3):
        grad_ref[r] = total[TRIALS * r : TRIALS * r + TRIALS, :]

    diagonal = lane == lax.broadcasted_iota(jnp.int32, (8, LANES), 0)

    def along_lanes(column):
        return jnp.sum(jnp.where(diagonal, column, 0.0), axis=0, keepdims=True)

    finite = jnp.where(lax.broadcasted_iota(jnp.int32, (8, 1), 0) < TRIALS, lowest, 0.0)
    lowest_ref[...] = along_lanes(finite)[0, :TRIALS]
    for copy in shares + sends + returns:
        copy.wait_send()

    row = finish_stage(row, dom_sum, flights, "dom", jnp.sum)
    energy = jnp.sum(jnp.where(mask, jnp.broadcast_to(row, (8, LANES)), 0.0), axis=1, keepdims=True)
    energy = energy / 3.0 / (nd * ns * chunks // 4 * LANES)
    energy_ref[...] = along_lanes(energy)[0, :TRIALS]


def copy_out(*refs):
    half = len(refs) // 2
    sems = refs[-1]
    copies = [pltpu.make_async_copy(refs[i], refs[half + i], sems.at[i]) for i in range(half)]
    for copy in copies:
        copy.start()
    for copy in copies:
        copy.wait()


def per_device(nd, ns, coords, direction, connect, shape_inv, weight, send_node, recv_slot):
    f32 = jnp.float32
    nodes = coords.shape[1]
    ghosts = send_node.shape[1]
    local = nodes + ghosts
    elems = connect.shape[1]
    per_row = elems // LANES
    chunks = 4 * per_row
    dma = pltpu.SemaphoreType.DMA
    any_space = pl.BlockSpec(memory_space=pl.ANY)
    vmem = pl.BlockSpec(memory_space=pltpu.VMEM)
    operands = (coords, direction, connect, shape_inv, weight.reshape(per_row, LANES), send_node, recv_slot)
    results = (
        jax.ShapeDtypeStruct((3, TRIALS, nodes), f32),
        jax.ShapeDtypeStruct((TRIALS,), f32),
        jax.ShapeDtypeStruct((TRIALS,), f32),
    )
    held = pl.pallas_call(
        functools.partial(kernel, nd, ns),
        out_shape=results,
        in_specs=[any_space] * 7,
        out_specs=(vmem,) * 3,
        scratch_shapes=[
            pltpu.VMEM((3, nodes), f32),
            pltpu.VMEM((3, nodes), f32),
            pltpu.VMEM((4, per_row, LANES), jnp.int32),
            pltpu.VMEM((9, per_row, LANES), f32),
            pltpu.VMEM((per_row, LANES), f32),
            pltpu.VMEM((1, ghosts), jnp.int32),
            pltpu.VMEM((1, ghosts), jnp.int32),
            pltpu.VMEM((8, ghosts), f32),
            pltpu.VMEM((4, 8, ghosts), f32),
            pltpu.VMEM((chunks, LANES), jnp.int32),
            pltpu.VMEM((local, 4 * elems), jnp.bfloat16),
            pltpu.VMEM((nodes, ghosts), jnp.bfloat16),
            pltpu.VMEM(((chunks + 1) * ROWS, LANES), f32),
            pltpu.VMEM((ROWS, ghosts), f32),
            pltpu.VMEM((4, ROWS, ghosts), f32),
            pltpu.VMEM((4, 1, LANES), f32),
            pltpu.VMEM((ns, LANES), f32),
            pltpu.VMEM((nd, LANES), f32),
            pltpu.VMEM((ns, LANES), f32),
            pltpu.VMEM((nd, LANES), f32),
            dma((21,)),
            dma((4,)),
            dma((4,)),
            dma((4,)),
            dma((4,)),
            dma((2, 2, ns - 1)),
            dma((2, 2, nd - 1)),
            pltpu.SemaphoreType.REGULAR((4,)),
        ],
        compiler_params=pltpu.CompilerParams(
            collective_id=0, has_side_effects=True, vmem_limit_bytes=1 << 24
        ),
        name="trial_energy",
    )(*(pltpu.with_memory_space_constraint(x, pltpu.HBM) for x in operands))
    gradient, energy, lowest = pl.pallas_call(
        copy_out,
        out_shape=results,
        in_specs=[vmem] * 3,
        out_specs=(any_space,) * 3,
        scratch_shapes=[dma((3,))],
        compiler_params=pltpu.CompilerParams(vmem_limit_bytes=1 << 20),
        name="copy_out",
    )(*held)
    return gradient.transpose(1, 0, 2), energy, lowest


def solution(mesh):
    placed = (
        P(None, ("dom", "sub")),
        P(None, ("dom", "sub")),
        P(None, ("dom", "sub")),
        P(None, ("dom", "sub")),
        P(("dom", "sub")),
        P(("dom", "sub"), None),
        P(("dom", "sub"), None),
    )
    return jax.shard_map(
        functools.partial(per_device, mesh.shape["dom"], mesh.shape["sub"]),
        mesh=mesh,
        in_specs=placed,
        out_specs=(P(None, None, ("dom", "sub")), P(), P()),
        check_vma=False,
    )
```

```python
import functools

import jax
import jax.numpy as jnp
from jax import lax
from jax.experimental import pallas as pl
from jax.experimental.pallas import tpu as pltpu
from jax.sharding import PartitionSpec as P

TRIALS = 4
LANES = 128
ROWS = 16
MESH = pl.DeviceIdType.MESH
step_scales = (1.0, 0.5, 0.25, 0.125)


def far_first(count, width=1):
    def far(j):
        x, y = j % width, j // width
        return min(x, width - x) + min(y, count // width - y)

    return sorted(range(1, count), key=lambda j: -far(j))


def take_lanes(table, index):
    return jnp.take_along_axis(table, index, axis=1, mode="promise_in_bounds")


def cofactor(m):
    return [
        [
            m[1][1] * m[2][2] - m[1][2] * m[2][1],
            m[1][2] * m[2][0] - m[1][0] * m[2][2],
            m[1][0] * m[2][1] - m[1][1] * m[2][0],
        ],
        [
            m[0][2] * m[2][1] - m[0][1] * m[2][2],
            m[0][0] * m[2][2] - m[0][2] * m[2][0],
            m[0][1] * m[2][0] - m[0][0] * m[2][1],
        ],
        [
            m[0][1] * m[1][2] - m[0][2] * m[1][1],
            m[0][2] * m[1][0] - m[0][0] * m[1][2],
            m[0][0] * m[1][1] - m[0][1] * m[1][0],
        ],
    ]


def split3(x):
    high = x.astype(jnp.bfloat16)
    rest = x - high.astype(jnp.float32)
    mid = rest.astype(jnp.bfloat16)
    low = (rest - mid.astype(jnp.float32)).astype(jnp.bfloat16)
    return jnp.concatenate([high, mid, low], axis=0)


def dot_nt(a, b):
    return lax.dot_general(a, b, (((1,), (1,)), ((), ())), preferred_element_type=jnp.float32)


def fold3(acc):
    return acc[:ROWS] + acc[ROWS : 2 * ROWS] + acc[2 * ROWS :]


def wait_all(like, sem):
    pltpu.make_async_copy(like, like, sem).wait()


def pack(values, op):
    lane = lax.broadcasted_iota(jnp.int32, (8, LANES), 1)
    half = [op(v, pltpu.roll(v, 64, 1)) for v in values]
    first = jnp.where(lane < 64, half[0], half[1])
    second = jnp.where(lane < 64, half[2], half[3])
    first = op(first, pltpu.roll(first, 32, 1))
    second = op(second, pltpu.roll(second, 96, 1))
    return jnp.where((lane // 32) % 2 == 1, first, second)


def unpack_mask():
    lane = lax.broadcasted_iota(jnp.int32, (8, LANES), 1)
    row = lax.broadcasted_iota(jnp.int32, (8, LANES), 0)
    group = lane // 32
    trial = jnp.where(group == 0, 2, jnp.where(group == 1, 0, jnp.where(group == 2, 3, 1)))
    return trial == row


def kernel(
    nd,
    ns,
    coords,
    direction,
    connect,
    shape_inv,
    weight,
    send_node,
    recv_slot,
    grad_ref,
    energy_ref,
    lowest_ref,
    co_v,
    di_v,
    con_v,
    inv_v,
    w_v,
    snd_v,
    rcv_v,
    out_tile,
    halo,
    idx_v,
    onehot,
    back_hot,
    cmat,
    gtile,
    gback,
    rows_v,
    sub_min,
    dom_min,
    sub_sum,
    dom_sum,
    in_sem,
    halo_sems,
    back_sems,
    sub_sems,
    dom_sems,
    known,
):
    f32 = jnp.float32
    d = lax.axis_index("dom")
    s = lax.axis_index("sub")
    nodes = co_v.shape[1]
    local = onehot.shape[0]
    chunks = con_v.shape[0] * 8

    loads = [
        pltpu.make_async_copy(coords, co_v, in_sem.at[0]),
        pltpu.make_async_copy(direction, di_v, in_sem.at[1]),
        pltpu.make_async_copy(send_node, snd_v, in_sem.at[2]),
        pltpu.make_async_copy(recv_slot, rcv_v, in_sem.at[3]),
        pltpu.make_async_copy(weight, w_v, in_sem.at[4]),
    ]
    wide = []
    for k in range(8):
        cut = pl.ds(k * LANES, LANES)
        wide.append(pltpu.make_async_copy(connect.at[:, cut], con_v.at[:, k, :], in_sem.at[5]))
        wide.append(pltpu.make_async_copy(shape_inv.at[:, cut], inv_v.at[:, k, :], in_sem.at[6]))
    for copy in loads[:3]:
        copy.start()

    barrier = pltpu.get_barrier_semaphore()
    for j in far_first(nd, 4):
        pl.semaphore_signal(barrier, inc=1, device_id=(lax.rem(d + j, nd), s), device_id_type=MESH)
    for j in (1, ns - 1):
        pl.semaphore_signal(barrier, inc=1, device_id=(d, lax.rem(s + j, ns)), device_id_type=MESH)
    for copy in loads[3:] + wide:
        copy.start()

    lane = lax.broadcasted_iota(jnp.int32, (8, LANES), 1)
    block = lane // 32
    for copy in loads[:3]:
        copy.wait()

    send_idx = jnp.broadcast_to(snd_v[...], (8, LANES))
    pad = jnp.zeros((2, nodes), f32)
    both = jnp.concatenate([co_v[...], di_v[...], pad], axis=0)
    picked = take_lanes(both[:, :LANES], send_idx & 127)
    for k in range(1, nodes // LANES):
        part = take_lanes(both[:, k * LANES : (k + 1) * LANES], send_idx & 127)
        picked = jnp.where(send_idx >= k * LANES, part, picked)
    out_tile[...] = picked

    pl.semaphore_wait(barrier, nd - 1 + 2)

    ahead = (
        (lax.rem(d + 1, nd), s),
        (lax.rem(d + nd - 1, nd), s),
        (d, lax.rem(s + 1, ns)),
        (d, lax.rem(s + ns - 1, ns)),
    )
    behind = (ahead[1], ahead[0], ahead[3], ahead[2])
    shares = [
        pltpu.make_async_remote_copy(
            src_ref=out_tile,
            dst_ref=halo.at[k],
            send_sem=halo_sems.at[0],
            recv_sem=halo_sems.at[1],
            device_id=ahead[k],
            device_id_type=MESH,
        )
        for k in range(4)
    ]
    for copy in shares:
        copy.start()

    for copy in loads[3:]:
        copy.wait()
    wait_all(con_v, in_sem.at[5])
    wait_all(inv_v, in_sem.at[6])

    slot_row = jnp.broadcast_to(rcv_v[...], (LANES, LANES))
    slot_hot = jnp.where(slot_row == lax.broadcasted_iota(jnp.int32, (LANES, LANES), 0), 1.0, 0.0).astype(jnp.bfloat16)
    arrival = dot_nt(lane.astype(f32).astype(jnp.bfloat16), slot_hot).astype(jnp.int32)
    corner = []
    for c in range(4):
        idx = con_v[c]
        ghost = idx >= nodes
        idx = jnp.where(ghost, nodes + take_lanes(arrival, jnp.where(ghost, idx - nodes, 0)), idx)
        idx_v[pl.ds(8 * c, 8), :] = idx
        corner.append(idx)

    owned = []
    for q in range(6):
        source = (co_v if q < 3 else di_v)
        r = q % 3
        per = []
        for c in range(4):
            low = corner[c] & 127
            value = take_lanes(jnp.broadcast_to(source[r : r + 1, :LANES], (8, LANES)), low)
            for k in range(1, nodes // LANES):
                part = take_lanes(
                    jnp.broadcast_to(source[r : r + 1, k * LANES : (k + 1) * LANES], (8, LANES)), low
                )
                value = jnp.where(corner[c] >= k * LANES, part, value)
            per.append(value)
        owned.append(per)

    send_row = jnp.broadcast_to(snd_v[...], (nodes, LANES))
    back_hot[...] = jnp.where(
        send_row == lax.broadcasted_iota(jnp.int32, (nodes, LANES), 0), 1.0, 0.0
    ).astype(jnp.bfloat16)

    wait_all(halo, halo_sems.at[1])
    reach = 2
    hops = []
    while reach < ns // 2:
        hops.append(reach)
        reach *= 2

    def greet(i):
        for j in (hops[i], ns - hops[i]):
            pl.semaphore_signal(known.at[i], inc=1, device_id=(d, lax.rem(s + j, ns)), device_id_type=MESH)

    if hops:
        greet(0)
    came = halo[0]
    for k in range(1, 4):
        came = jnp.where(block == k, halo[k], came)

    values = []
    for q in range(6):
        row = jnp.broadcast_to(came[q : q + 1, :], (8, LANES))
        values.append(
            [jnp.where(corner[c] >= nodes, take_lanes(row, corner[c] & 127), owned[q][c]) for c in range(4)]
        )
    w9 = [inv_v[i] for i in range(9)]

    def edges_times_inverse(base):
        out = []
        for r in range(3):
            edge = [values[base + r][c] - values[base + r][0] for c in (1, 2, 3)]
            out.append([edge[0] * w9[m] + edge[1] * w9[3 + m] + edge[2] * w9[6 + m] for m in range(3)])
        return out

    jac_x = edges_times_inverse(0)
    jac_d = edges_times_inverse(3)
    jacs = []
    cofs = []
    dets = []
    for t in range(TRIALS):
        a = step_scales[t]
        m = [[jac_x[r][k] + a * jac_d[r][k] for k in range(3)] for r in range(3)]
        cof = cofactor(m)
        jacs.append(m)
        cofs.append(cof)
        dets.append(m[0][0] * cof[0][0] + m[0][1] * cof[0][1] + m[0][2] * cof[0][2])

    def start_stage(row, buf, sems, axis):
        me, count = (s, ns) if axis == "sub" else (d, nd)
        copies = []
        for j in far_first(count, 1 if axis == "sub" else 4):
            peer = lax.rem(me + j, count)
            copies.append(
                pltpu.make_async_remote_copy(
                    src_ref=row,
                    dst_ref=buf.at[pl.ds(me, 1), :],
                    send_sem=sems.at[0],
                    recv_sem=sems.at[1],
                    device_id=(d, peer) if axis == "sub" else (peer, s),
                    device_id_type=MESH,
                )
            )
        for copy in copies:
            copy.start()

    def finish_stage(row, buf, sems, axis, reduce):
        me, count = (s, ns) if axis == "sub" else (d, nd)
        wait_all(buf.at[pl.ds(0, count - 1), :], sems.at[1])
        mine = lax.broadcasted_iota(jnp.int32, (count, LANES), 0) == me
        return reduce(jnp.where(mine, row, buf[...]), axis=0, keepdims=True)

    def build_hot(first, last):
        node = lax.broadcasted_iota(jnp.int32, (local, LANES), 0)

        def step(j, carry):
            row = jnp.broadcast_to(idx_v[pl.ds(j, 1), :], (local, LANES))
            onehot[:, pl.ds(pl.multiple_of(j * LANES, LANES), LANES)] = jnp.where(row == node, 1.0, 0.0).astype(
                jnp.bfloat16
            )
            return carry

        lax.fori_loop(first, last, step, 0)

    row = jnp.min(pack(dets, jnp.minimum), axis=0, keepdims=True)
    rows_v[0] = row
    start_stage(rows_v.at[0], dom_min, dom_sems.at[0], "dom")
    weights = w_v[...]
    squares = []
    for t in range(TRIALS):
        total = jacs[t][0][0] * jacs[t][0][0]
        for r in range(3):
            for k in range(3):
                if r + k > 0:
                    total = total + jacs[t][r][k] * jacs[t][r][k]
        squares.append(weights * total)
    build_hot(0, chunks // 2)
    for i in range(len(hops)):
        pl.semaphore_wait(known.at[i], 2)
        if i + 1 < len(hops):
            greet(i + 1)
    row = finish_stage(row, dom_min, dom_sems.at[0], "dom", jnp.min)
    rows_v[1] = row
    start_stage(rows_v.at[1], sub_min, sub_sems.at[0], "sub")
    build_hot(chunks // 2, chunks)
    row = finish_stage(row, sub_min, sub_sems.at[0], "sub", jnp.min)

    mask = unpack_mask()
    lowest = jnp.min(jnp.where(mask, jnp.broadcast_to(row, (8, LANES)), jnp.inf), axis=1, keepdims=True)
    shift = lowest - 1.0 - jnp.abs(lowest)

    energies = []
    scale_jac = []
    scale_cof = []
    for t in range(TRIALS):
        lifted = dets[t] - jnp.broadcast_to(shift[t : t + 1, :], (8, LANES))
        power = jnp.exp(jnp.log(lifted) * (-2.0 / 3.0))
        energy = squares[t] * power
        energies.append(energy)
        scale_jac.append(weights * power * (2.0 / 3.0))
        scale_cof.append(energy / lifted * (2.0 / 9.0))

    row = jnp.sum(pack(energies, jnp.add), axis=0, keepdims=True)
    rows_v[2] = row
    start_stage(rows_v.at[2], sub_sum, sub_sems.at[1], "sub")

    for t in range(TRIALS):
        for r in range(3):
            g = [scale_jac[t] * jacs[t][r][k] - scale_cof[t] * cofs[t][r][k] for k in range(3)]
            h = [g[0] * w9[3 * e] + g[1] * w9[3 * e + 1] + g[2] * w9[3 * e + 2] for e in range(3)]
            h = [-(h[0] + h[1] + h[2])] + h
            for c in range(4):
                cmat[pl.ds(8 * ROWS * c + TRIALS * r + t, 8, stride=ROWS), :] = h[c]

    def scatter_step(j, acc):
        pair = [split3(cmat[pl.ds(pl.multiple_of((2 * j + i) * ROWS, ROWS), ROWS), :]) for i in range(2)]
        left = jnp.concatenate(pair, axis=1)
        right = onehot[:, pl.ds(pl.multiple_of(j * 2 * LANES, LANES), 2 * LANES)]
        return acc + dot_nt(left, right)

    summed = fold3(lax.fori_loop(0, chunks // 2, scatter_step, jnp.zeros((3 * ROWS, local), f32)))
    gtile[...] = summed[:, nodes:]
    returns = [
        pltpu.make_async_remote_copy(
            src_ref=gtile,
            dst_ref=gback.at[k],
            send_sem=back_sems.at[0],
            recv_sem=back_sems.at[1],
            device_id=behind[k],
            device_id_type=MESH,
        )
        for k in range(4)
    ]
    for copy in returns:
        copy.start()

    row = finish_stage(row, sub_sum, sub_sems.at[1], "sub", jnp.sum)
    rows_v[3] = row
    start_stage(rows_v.at[3], dom_sum, dom_sems.at[1], "dom")

    wait_all(gback, back_sems.at[1])
    wide_block = lax.broadcasted_iota(jnp.int32, (ROWS, LANES), 1) // 32
    came = gback[0]
    for k in range(1, 4):
        came = jnp.where(wide_block == k, gback[k], came)
    total = summed[:, :nodes] + fold3(dot_nt(split3(came), back_hot[...]))
    for r in range(3):
        grad_ref[r] = total[TRIALS * r : TRIALS * r + TRIALS, :]

    diagonal = lane == lax.broadcasted_iota(jnp.int32, (8, LANES), 0)

    def along_lanes(column):
        return jnp.sum(jnp.where(diagonal, column, 0.0), axis=0, keepdims=True)

    finite = jnp.where(lax.broadcasted_iota(jnp.int32, (8, 1), 0) < TRIALS, lowest, 0.0)
    lowest_ref[...] = along_lanes(finite)[0, :TRIALS]
    wait_all(halo, halo_sems.at[0])
    wait_all(gback, back_sems.at[0])
    for i in range(2):
        wait_all(sub_min.at[pl.ds(0, ns - 1), :], sub_sems.at[i, 0])
        wait_all(dom_min.at[pl.ds(0, nd - 1), :], dom_sems.at[i, 0])

    row = finish_stage(row, dom_sum, dom_sems.at[1], "dom", jnp.sum)
    energy = jnp.sum(jnp.where(mask, jnp.broadcast_to(row, (8, LANES)), 0.0), axis=1, keepdims=True)
    energy = energy / 3.0 / (nd * ns * chunks // 4 * LANES)
    energy_ref[...] = along_lanes(energy)[0, :TRIALS]


def copy_out(*refs):
    half = len(refs) // 2
    sems = refs[-1]
    copies = [pltpu.make_async_copy(refs[i], refs[half + i], sems.at[i]) for i in range(half)]
    for copy in copies:
        copy.start()
    for copy in copies:
        copy.wait()


def per_device(nd, ns, coords, direction, connect, shape_inv, weight, send_node, recv_slot):
    f32 = jnp.float32
    nodes = coords.shape[1]
    ghosts = send_node.shape[1]
    local = nodes + ghosts
    elems = connect.shape[1]
    per_row = elems // LANES
    chunks = 4 * per_row
    dma = pltpu.SemaphoreType.DMA
    any_space = pl.BlockSpec(memory_space=pl.ANY)
    vmem = pl.BlockSpec(memory_space=pltpu.VMEM)
    operands = (coords, direction, connect, shape_inv, weight.reshape(per_row, LANES), send_node, recv_slot)
    results = (
        jax.ShapeDtypeStruct((3, TRIALS, nodes), f32),
        jax.ShapeDtypeStruct((TRIALS,), f32),
        jax.ShapeDtypeStruct((TRIALS,), f32),
    )
    held = pl.pallas_call(
        functools.partial(kernel, nd, ns),
        out_shape=results,
        in_specs=[any_space] * 7,
        out_specs=(vmem,) * 3,
        scratch_shapes=[
            pltpu.VMEM((3, nodes), f32),
            pltpu.VMEM((3, nodes), f32),
            pltpu.VMEM((4, per_row, LANES), jnp.int32),
            pltpu.VMEM((9, per_row, LANES), f32),
            pltpu.VMEM((per_row, LANES), f32),
            pltpu.VMEM((1, ghosts), jnp.int32),
            pltpu.VMEM((1, ghosts), jnp.int32),
            pltpu.VMEM((8, ghosts), f32),
            pltpu.VMEM((4, 8, ghosts), f32),
            pltpu.VMEM((chunks, LANES), jnp.int32),
            pltpu.VMEM((local, 4 * elems), jnp.bfloat16),
            pltpu.VMEM((nodes, ghosts), jnp.bfloat16),
            pltpu.VMEM(((chunks + 1) * ROWS, LANES), f32),
            pltpu.VMEM((ROWS, ghosts), f32),
            pltpu.VMEM((4, ROWS, ghosts), f32),
            pltpu.VMEM((4, 1, LANES), f32),
            pltpu.VMEM((ns, LANES), f32),
            pltpu.VMEM((nd, LANES), f32),
            pltpu.VMEM((ns, LANES), f32),
            pltpu.VMEM((nd, LANES), f32),
            dma((7,)),
            dma((2,)),
            dma((2,)),
            dma((2, 2)),
            dma((2, 2)),
            pltpu.SemaphoreType.REGULAR((2,)),
        ],
        compiler_params=pltpu.CompilerParams(
            collective_id=0, has_side_effects=True, vmem_limit_bytes=1 << 24
        ),
        name="trial_energy",
    )(*(pltpu.with_memory_space_constraint(x, pltpu.HBM) for x in operands))
    gradient, energy, lowest = pl.pallas_call(
        copy_out,
        out_shape=results,
        in_specs=[vmem] * 3,
        out_specs=(any_space,) * 3,
        scratch_shapes=[dma((3,))],
        compiler_params=pltpu.CompilerParams(vmem_limit_bytes=1 << 20),
        name="copy_out",
    )(*held)
    return gradient.transpose(1, 0, 2), energy, lowest


def solution(mesh):
    placed = (
        P(None, ("dom", "sub")),
        P(None, ("dom", "sub")),
        P(None, ("dom", "sub")),
        P(None, ("dom", "sub")),
        P(("dom", "sub")),
        P(("dom", "sub"), None),
        P(("dom", "sub"), None),
    )
    return jax.shard_map(
        functools.partial(per_device, mesh.shape["dom"], mesh.shape["sub"]),
        mesh=mesh,
        in_specs=placed,
        out_specs=(P(None, None, ("dom", "sub")), P(), P()),
        check_vma=False,
    )
```

```python
import functools

import jax
import jax.numpy as jnp
from jax import lax
from jax.experimental import pallas as pl
from jax.experimental.pallas import tpu as pltpu
from jax.sharding import PartitionSpec as P

TRIALS = 4
LANES = 128
ROWS = 16
MESH = pl.DeviceIdType.MESH
step_scales = (1.0, 0.5, 0.25, 0.125)


def far_first(count, width=1):
    def far(j):
        x, y = j % width, j // width
        return min(x, width - x) + min(y, count // width - y)

    return sorted(range(1, count), key=lambda j: -far(j))


def take_lanes(table, index):
    return jnp.take_along_axis(table, index, axis=1, mode="promise_in_bounds")


def cofactor(m):
    return [
        [
            m[1][1] * m[2][2] - m[1][2] * m[2][1],
            m[1][2] * m[2][0] - m[1][0] * m[2][2],
            m[1][0] * m[2][1] - m[1][1] * m[2][0],
        ],
        [
            m[0][2] * m[2][1] - m[0][1] * m[2][2],
            m[0][0] * m[2][2] - m[0][2] * m[2][0],
            m[0][1] * m[2][0] - m[0][0] * m[2][1],
        ],
        [
            m[0][1] * m[1][2] - m[0][2] * m[1][1],
            m[0][2] * m[1][0] - m[0][0] * m[1][2],
            m[0][0] * m[1][1] - m[0][1] * m[1][0],
        ],
    ]


def split3(x):
    high = x.astype(jnp.bfloat16)
    rest = x - high.astype(jnp.float32)
    mid = rest.astype(jnp.bfloat16)
    low = (rest - mid.astype(jnp.float32)).astype(jnp.bfloat16)
    return jnp.concatenate([high, mid, low], axis=0)


def dot_nt(a, b):
    return lax.dot_general(a, b, (((1,), (1,)), ((), ())), preferred_element_type=jnp.float32)


def fold3(acc):
    return acc[:ROWS] + acc[ROWS : 2 * ROWS] + acc[2 * ROWS :]


def wait_all(like, sem):
    pltpu.make_async_copy(like, like, sem).wait()


def pack(values, reduce):
    lane = lax.broadcasted_iota(jnp.int32, (8, LANES), 1)
    columns = [reduce(v, axis=1, keepdims=True) for v in values]
    both = jnp.where(lane == 0, columns[0], jnp.where(lane == 1, columns[1], jnp.where(lane == 2, columns[2], columns[3])))
    return reduce(both, axis=0, keepdims=True)


def kernel(
    nd,
    ns,
    coords,
    direction,
    connect,
    shape_inv,
    weight,
    send_node,
    recv_slot,
    grad_ref,
    energy_ref,
    lowest_ref,
    co_v,
    di_v,
    con_v,
    inv_v,
    w_v,
    snd_v,
    rcv_v,
    out_tile,
    halo,
    idx_v,
    onehot,
    back_hot,
    cmat,
    gtile,
    gback,
    rows_v,
    sub_min,
    dom_min,
    sub_sum,
    dom_sum,
    in_sem,
    halo_sems,
    back_sems,
    sub_sems,
    dom_sems,
    known,
):
    f32 = jnp.float32
    d = lax.axis_index("dom")
    s = lax.axis_index("sub")
    nodes = co_v.shape[1]
    local = onehot.shape[0]
    chunks = con_v.shape[0] * 8

    loads = [
        pltpu.make_async_copy(coords, co_v, in_sem.at[0]),
        pltpu.make_async_copy(direction, di_v, in_sem.at[1]),
        pltpu.make_async_copy(send_node, snd_v, in_sem.at[2]),
        pltpu.make_async_copy(recv_slot, rcv_v, in_sem.at[3]),
        pltpu.make_async_copy(weight, w_v, in_sem.at[4]),
    ]
    wide = []
    for k in range(8):
        cut = pl.ds(k * LANES, LANES)
        wide.append(pltpu.make_async_copy(connect.at[:, cut], con_v.at[:, k, :], in_sem.at[5]))
        wide.append(pltpu.make_async_copy(shape_inv.at[:, cut], inv_v.at[:, k, :], in_sem.at[6]))
    for copy in loads[:3]:
        copy.start()

    barrier = pltpu.get_barrier_semaphore()
    for j in far_first(nd, 4):
        pl.semaphore_signal(barrier, inc=1, device_id=(lax.rem(d + j, nd), s), device_id_type=MESH)
    for j in (1, ns - 1):
        pl.semaphore_signal(barrier, inc=1, device_id=(d, lax.rem(s + j, ns)), device_id_type=MESH)
    for copy in loads[3:] + wide:
        copy.start()

    lane = lax.broadcasted_iota(jnp.int32, (8, LANES), 1)
    block = lane // 32
    for copy in loads[:3]:
        copy.wait()

    send_idx = jnp.broadcast_to(snd_v[...], (8, LANES))
    pad = jnp.zeros((2, nodes), f32)
    both = jnp.concatenate([co_v[...], di_v[...], pad], axis=0)
    picked = take_lanes(both[:, :LANES], send_idx & 127)
    for k in range(1, nodes // LANES):
        part = take_lanes(both[:, k * LANES : (k + 1) * LANES], send_idx & 127)
        picked = jnp.where(send_idx >= k * LANES, part, picked)
    out_tile[...] = picked

    pl.semaphore_wait(barrier, nd - 1 + 2)

    ahead = (
        (lax.rem(d + 1, nd), s),
        (lax.rem(d + nd - 1, nd), s),
        (d, lax.rem(s + 1, ns)),
        (d, lax.rem(s + ns - 1, ns)),
    )
    behind = (ahead[1], ahead[0], ahead[3], ahead[2])
    shares = [
        pltpu.make_async_remote_copy(
            src_ref=out_tile,
            dst_ref=halo.at[k],
            send_sem=halo_sems.at[0],
            recv_sem=halo_sems.at[1],
            device_id=ahead[k],
            device_id_type=MESH,
        )
        for k in range(4)
    ]
    for copy in shares:
        copy.start()

    for copy in loads[3:]:
        copy.wait()
    wait_all(con_v, in_sem.at[5])
    wait_all(inv_v, in_sem.at[6])

    slot_row = jnp.broadcast_to(rcv_v[...], (LANES, LANES))
    slot_hot = jnp.where(slot_row == lax.broadcasted_iota(jnp.int32, (LANES, LANES), 0), 1.0, 0.0).astype(jnp.bfloat16)
    arrival = dot_nt(lane.astype(f32).astype(jnp.bfloat16), slot_hot).astype(jnp.int32)
    corner = []
    for c in range(4):
        idx = con_v[c]
        ghost = idx >= nodes
        idx = jnp.where(ghost, nodes + take_lanes(arrival, jnp.where(ghost, idx - nodes, 0)), idx)
        idx_v[pl.ds(8 * c, 8), :] = idx
        corner.append(idx)

    owned = []
    for q in range(6):
        source = (co_v if q < 3 else di_v)
        r = q % 3
        per = []
        for c in range(4):
            low = corner[c] & 127
            value = take_lanes(jnp.broadcast_to(source[r : r + 1, :LANES], (8, LANES)), low)
            for k in range(1, nodes // LANES):
                part = take_lanes(
                    jnp.broadcast_to(source[r : r + 1, k * LANES : (k + 1) * LANES], (8, LANES)), low
                )
                value = jnp.where(corner[c] >= k * LANES, part, value)
            per.append(value)
        owned.append(per)

    send_row = jnp.broadcast_to(snd_v[...], (nodes, LANES))
    back_hot[...] = jnp.where(
        send_row == lax.broadcasted_iota(jnp.int32, (nodes, LANES), 0), 1.0, 0.0
    ).astype(jnp.bfloat16)

    wait_all(halo, halo_sems.at[1])
    reach = 2
    hops = []
    while reach < ns // 2:
        hops.append(reach)
        reach *= 2

    def greet(i):
        for j in (hops[i], ns - hops[i]):
            pl.semaphore_signal(known.at[i], inc=1, device_id=(d, lax.rem(s + j, ns)), device_id_type=MESH)

    if hops:
        greet(0)
    came = halo[0]
    for k in range(1, 4):
        came = jnp.where(block == k, halo[k], came)

    values = []
    for q in range(6):
        row = jnp.broadcast_to(came[q : q + 1, :], (8, LANES))
        values.append(
            [jnp.where(corner[c] >= nodes, take_lanes(row, corner[c] & 127), owned[q][c]) for c in range(4)]
        )
    w9 = [inv_v[i] for i in range(9)]

    def edges_times_inverse(base):
        out = []
        for r in range(3):
            edge = [values[base + r][c] - values[base + r][0] for c in (1, 2, 3)]
            out.append([edge[0] * w9[m] + edge[1] * w9[3 + m] + edge[2] * w9[6 + m] for m in range(3)])
        return out

    jac_x = edges_times_inverse(0)
    jac_d = edges_times_inverse(3)
    jacs = []
    cofs = []
    dets = []
    for t in range(TRIALS):
        a = step_scales[t]
        m = [[jac_x[r][k] + a * jac_d[r][k] for k in range(3)] for r in range(3)]
        cof = cofactor(m)
        jacs.append(m)
        cofs.append(cof)
        dets.append(m[0][0] * cof[0][0] + m[0][1] * cof[0][1] + m[0][2] * cof[0][2])

    def start_stage(row, buf, sems, axis):
        me, count = (s, ns) if axis == "sub" else (d, nd)
        copies = []
        for j in far_first(count, 1 if axis == "sub" else 4):
            peer = lax.rem(me + j, count)
            copies.append(
                pltpu.make_async_remote_copy(
                    src_ref=row,
                    dst_ref=buf.at[pl.ds(me, 1), :],
                    send_sem=sems.at[0],
                    recv_sem=sems.at[1],
                    device_id=(d, peer) if axis == "sub" else (peer, s),
                    device_id_type=MESH,
                )
            )
        for copy in copies:
            copy.start()

    def finish_stage(row, buf, sems, axis, reduce):
        me, count = (s, ns) if axis == "sub" else (d, nd)
        wait_all(buf.at[pl.ds(0, count - 1), :], sems.at[1])
        mine = lax.broadcasted_iota(jnp.int32, (count, LANES), 0) == me
        return reduce(jnp.where(mine, row, buf[...]), axis=0, keepdims=True)

    def build_hot(first, last):
        node = lax.broadcasted_iota(jnp.int32, (local, LANES), 0)

        def step(j, carry):
            row = jnp.broadcast_to(idx_v[pl.ds(j, 1), :], (local, LANES))
            onehot[:, pl.ds(pl.multiple_of(j * LANES, LANES), LANES)] = jnp.where(row == node, 1.0, 0.0).astype(
                jnp.bfloat16
            )
            return carry

        lax.fori_loop(first, last, step, 0)

    row = pack(dets, jnp.min)
    rows_v[0] = row
    start_stage(rows_v.at[0], dom_min, dom_sems.at[0], "dom")
    weights = w_v[...]
    squares = []
    for t in range(TRIALS):
        total = jacs[t][0][0] * jacs[t][0][0]
        for r in range(3):
            for k in range(3):
                if r + k > 0:
                    total = total + jacs[t][r][k] * jacs[t][r][k]
        squares.append(weights * total)
    build_hot(0, chunks // 2)
    for i in range(len(hops)):
        pl.semaphore_wait(known.at[i], 2)
        if i + 1 < len(hops):
            greet(i + 1)
    row = finish_stage(row, dom_min, dom_sems.at[0], "dom", jnp.min)
    rows_v[1] = row
    start_stage(rows_v.at[1], sub_min, sub_sems.at[0], "sub")
    build_hot(chunks // 2, chunks)
    row = finish_stage(row, sub_min, sub_sems.at[0], "sub", jnp.min)

    lowest = row
    shift = lowest - 1.0 - jnp.abs(lowest)

    energies = []
    scale_jac = []
    scale_cof = []
    for t in range(TRIALS):
        lifted = dets[t] - jnp.broadcast_to(shift[:, t : t + 1], (8, LANES))
        power = jnp.exp(jnp.log(lifted) * (-2.0 / 3.0))
        energy = squares[t] * power
        energies.append(energy)
        scale_jac.append(weights * power * (2.0 / 3.0))
        scale_cof.append(energy / lifted * (2.0 / 9.0))

    row = pack(energies, jnp.sum)
    rows_v[2] = row
    start_stage(rows_v.at[2], sub_sum, sub_sems.at[1], "sub")

    for t in range(TRIALS):
        for r in range(3):
            g = [scale_jac[t] * jacs[t][r][k] - scale_cof[t] * cofs[t][r][k] for k in range(3)]
            h = [g[0] * w9[3 * e] + g[1] * w9[3 * e + 1] + g[2] * w9[3 * e + 2] for e in range(3)]
            h = [-(h[0] + h[1] + h[2])] + h
            for c in range(4):
                cmat[pl.ds(8 * ROWS * c + TRIALS * r + t, 8, stride=ROWS), :] = h[c]

    def scatter_step(j, acc):
        pair = [split3(cmat[pl.ds(pl.multiple_of((2 * j + i) * ROWS, ROWS), ROWS), :]) for i in range(2)]
        left = jnp.concatenate(pair, axis=1)
        right = onehot[:, pl.ds(pl.multiple_of(j * 2 * LANES, LANES), 2 * LANES)]
        return acc + dot_nt(left, right)

    summed = fold3(lax.fori_loop(0, chunks // 2, scatter_step, jnp.zeros((3 * ROWS, local), f32)))
    gtile[...] = summed[:, nodes:]
    returns = [
        pltpu.make_async_remote_copy(
            src_ref=gtile,
            dst_ref=gback.at[k],
            send_sem=back_sems.at[0],
            recv_sem=back_sems.at[1],
            device_id=behind[k],
            device_id_type=MESH,
        )
        for k in range(4)
    ]
    for copy in returns:
        copy.start()

    row = finish_stage(row, sub_sum, sub_sems.at[1], "sub", jnp.sum)
    rows_v[3] = row
    start_stage(rows_v.at[3], dom_sum, dom_sems.at[1], "dom")

    wait_all(gback, back_sems.at[1])
    wide_block = lax.broadcasted_iota(jnp.int32, (ROWS, LANES), 1) // 32
    came = gback[0]
    for k in range(1, 4):
        came = jnp.where(wide_block == k, gback[k], came)
    total = summed[:, :nodes] + fold3(dot_nt(split3(came), back_hot[...]))
    for r in range(3):
        grad_ref[r] = total[TRIALS * r : TRIALS * r + TRIALS, :]

    lowest_ref[...] = lowest[0, :TRIALS]
    wait_all(halo, halo_sems.at[0])
    wait_all(gback, back_sems.at[0])
    for i in range(2):
        wait_all(sub_min.at[pl.ds(0, ns - 1), :], sub_sems.at[i, 0])
        wait_all(dom_min.at[pl.ds(0, nd - 1), :], dom_sems.at[i, 0])

    row = finish_stage(row, dom_sum, dom_sems.at[1], "dom", jnp.sum)
    energy = row / 3.0 / (nd * ns * chunks // 4 * LANES)
    energy_ref[...] = energy[0, :TRIALS]


def copy_out(*refs):
    half = len(refs) // 2
    sems = refs[-1]
    copies = [pltpu.make_async_copy(refs[i], refs[half + i], sems.at[i]) for i in range(half)]
    for copy in copies:
        copy.start()
    for copy in copies:
        copy.wait()


def per_device(nd, ns, coords, direction, connect, shape_inv, weight, send_node, recv_slot):
    f32 = jnp.float32
    nodes = coords.shape[1]
    ghosts = send_node.shape[1]
    local = nodes + ghosts
    elems = connect.shape[1]
    per_row = elems // LANES
    chunks = 4 * per_row
    dma = pltpu.SemaphoreType.DMA
    any_space = pl.BlockSpec(memory_space=pl.ANY)
    vmem = pl.BlockSpec(memory_space=pltpu.VMEM)
    operands = (coords, direction, connect, shape_inv, weight.reshape(per_row, LANES), send_node, recv_slot)
    results = (
        jax.ShapeDtypeStruct((3, TRIALS, nodes), f32),
        jax.ShapeDtypeStruct((TRIALS,), f32),
        jax.ShapeDtypeStruct((TRIALS,), f32),
    )
    held = pl.pallas_call(
        functools.partial(kernel, nd, ns),
        out_shape=results,
        in_specs=[any_space] * 7,
        out_specs=(vmem,) * 3,
        scratch_shapes=[
            pltpu.VMEM((3, nodes), f32),
            pltpu.VMEM((3, nodes), f32),
            pltpu.VMEM((4, per_row, LANES), jnp.int32),
            pltpu.VMEM((9, per_row, LANES), f32),
            pltpu.VMEM((per_row, LANES), f32),
            pltpu.VMEM((1, ghosts), jnp.int32),
            pltpu.VMEM((1, ghosts), jnp.int32),
            pltpu.VMEM((8, ghosts), f32),
            pltpu.VMEM((4, 8, ghosts), f32),
            pltpu.VMEM((chunks, LANES), jnp.int32),
            pltpu.VMEM((local, 4 * elems), jnp.bfloat16),
            pltpu.VMEM((nodes, ghosts), jnp.bfloat16),
            pltpu.VMEM(((chunks + 1) * ROWS, LANES), f32),
            pltpu.VMEM((ROWS, ghosts), f32),
            pltpu.VMEM((4, ROWS, ghosts), f32),
            pltpu.VMEM((4, 1, LANES), f32),
            pltpu.VMEM((ns, LANES), f32),
            pltpu.VMEM((nd, LANES), f32),
            pltpu.VMEM((ns, LANES), f32),
            pltpu.VMEM((nd, LANES), f32),
            dma((7,)),
            dma((2,)),
            dma((2,)),
            dma((2, 2)),
            dma((2, 2)),
            pltpu.SemaphoreType.REGULAR((2,)),
        ],
        compiler_params=pltpu.CompilerParams(
            collective_id=0, has_side_effects=True, vmem_limit_bytes=1 << 24
        ),
        name="trial_energy",
    )(*(pltpu.with_memory_space_constraint(x, pltpu.HBM) for x in operands))
    gradient, energy, lowest = pl.pallas_call(
        copy_out,
        out_shape=results,
        in_specs=[vmem] * 3,
        out_specs=(any_space,) * 3,
        scratch_shapes=[dma((3,))],
        compiler_params=pltpu.CompilerParams(vmem_limit_bytes=1 << 20),
        name="copy_out",
    )(*held)
    return gradient.transpose(1, 0, 2), energy, lowest


def solution(mesh):
    placed = (
        P(None, ("dom", "sub")),
        P(None, ("dom", "sub")),
        P(None, ("dom", "sub")),
        P(None, ("dom", "sub")),
        P(("dom", "sub")),
        P(("dom", "sub"), None),
        P(("dom", "sub"), None),
    )
    return jax.shard_map(
        functools.partial(per_device, mesh.shape["dom"], mesh.shape["sub"]),
        mesh=mesh,
        in_specs=placed,
        out_specs=(P(None, None, ("dom", "sub")), P(), P()),
        check_vma=False,
    )
```
